128 devices in a mesh: mech: 16 (over x, z), bin: 8 (over y, core).
Axes of the slice: x: 4, y: 4, z: 4, core: 2. Of those that a mesh axis runs over, the one named last changes fastest.
Arguments:
- face_coords: float32 [27, 262144], P(None, ('mech', 'bin')), may hold values from -1.03 to 1.03, as said below
- face_stiff: float32 [262144], P(('mech', 'bin')), may hold values from 1 to 10
- bin_order: int32 [128, 2048], P(('mech', 'bin')), may hold values from 0 to 2047, each once within a row
- slave_pos: float32 [3, 524288], P(None, ('mech', 'bin')), may hold values from -1.3 to 1.3, as said below
- slave_dest: int32 [524288, 1], P(('mech', 'bin')), may hold values from 0 to 127, as said below
- face_slot: int32 [524288], P(('mech', 'bin')), may hold values from 0 to 2047
- block_count: int32 [128, 32], P(('mech', 'bin')), may hold values from 64 to 128
- mirror_face: int32 [262144], P(('mech', 'bin')), may hold values from 0 to 2047
- mirror_node: int32 [262144], P(('mech', 'bin')), may hold values from 0 to 8
- mirror_dest: int32 [262144, 1], P(('mech', 'bin')), may hold values from 0 to 127, as said below
- mirror_slot: int32 [262144], P(('mech', 'bin')), may hold values from 0 to 2047
Outputs:
- slave_force: float32 [3, 524288], P(None, ('mech', 'bin'))
- face_force: float32 [27, 262144], P(None, ('mech', 'bin'))
The draws below stay inside these ranges and needn't reach their ends.
Inputs may be any that keep to these rules, and one draw needn't show every extreme that they name: `face_coords`: node a = i + 3 j of every face lies within 0.03 of (i - 1, j - 1) in its first two components; its third component lies in -0.35 to 0.35. `slave_pos`: first two components lie in -1.3 to 1.3, the third in -0.6 to 0.6. `slave_dest`: among the rows of one device, no bin device is named by more than 64 rows, no element owner holds the named faces of more than 64 rows, and no bin device together with one owner by more than 64 // 8 rows; some bin device and some owner reach 64 from every device. `mirror_dest`: among the rows of one device, no partner device is named by more than 32 rows, no element owner holds the named faces of more than 32 rows, and no partner device together with one owner by more than 32 // 8 rows; some partner device and some owner reach 32 from every device. `bin_order`: each row is a permutation of 0 to 2047.
All inputs are finite; a program needn't handle non-finite values.
Results may differ from the reference program's by a relative error of at most 0.0003.
Values sent between devices are 32-bit elements; how exact they have to be, the bound alone decides.
No kernel may reach another device: no remote copies, remote signals or barrier semaphores. Data moves between devices by JAX's collectives and lax.ppermute only.
A program may use at most 64 MiB of HBM per device.

```python
import math
import jax
import jax.numpy as jnp
from jax import lax

F_DEV = 2048
S_DEV = 4096
M_DEV = 2048
NEWTON = 5
FACES = 262144
NODES = 524288
MIRRORS = 262144
SLOT_CAP = 64
MIRROR_CAP = 32
N_MECH = 16
N_BIN = 8
DEVICES = 128


def draw_face_coords(key, part):
    key_plane, key_height = jax.random.split(key, 2)
    entry = jnp.arange(27, dtype=jnp.int32)
    node_id = entry // 3
    component = entry % 3
    grid_x = (node_id % 3 - 1).astype(jnp.float32)
    grid_y = (node_id // 3 - 1).astype(jnp.float32)
    base = jnp.where(component == 0, grid_x, jnp.where(component == 1, grid_y, 0.0))
    planar = jax.random.uniform(key_plane, (27, FACES), jnp.float32, -0.03, 0.03)
    height = jax.random.uniform(key_height, (27, FACES), jnp.float32, -0.35, 0.35)
    values = jnp.where((component == 2)[:, None], height, base[:, None] + planar)
    return values.astype(jnp.float32)


def draw_slave_pos(key, part):
    key_plane, key_depth, key_beyond, key_select = jax.random.split(key, 4)
    plane = jax.random.uniform(key_plane, (2, NODES), jnp.float32, -1.0, 1.0)
    depth = jax.random.uniform(key_depth, (1, NODES), jnp.float32, -0.6, 0.6)
    beyond = jax.random.uniform(key_beyond, (2, NODES), jnp.float32, 1.15, 1.3)
    selected = jax.random.uniform(key_select, (2, NODES), jnp.float32) < 0.02
    plane = jnp.where(selected, jnp.sign(plane) * beyond, plane)
    return jnp.concatenate([plane, depth], 0).astype(jnp.float32)


def pair_layout(key, rows, capacity):
    cell_cap = capacity // N_BIN
    slot_total = DEVICES * capacity
    block_faces = F_DEV // N_BIN
    key_hot, key_source = jax.random.split(key)
    hot_pick = jax.random.randint(key_hot, (2,), 0, DEVICES)
    slot_ids = jnp.arange(slot_total, dtype=jnp.int32)
    cell_id = slot_ids // cell_cap
    dest_dev = cell_id // N_BIN
    face_block = cell_id % N_BIN
    owner_dev = dest_dev // N_BIN * N_BIN + face_block
    forced = ((dest_dev == hot_pick[0]) | (owner_dev == hot_pick[1])).astype(jnp.int32)

    def per_source(source):
        own_key = jax.random.fold_in(key_source, source)
        key_rank, key_rows, key_face = jax.random.split(own_key, 3)
        ranking = jax.random.permutation(key_rank, slot_total).astype(jnp.int32)
        scores = ranking + forced * slot_total
        chosen = lax.top_k(scores, rows)[1]
        chosen = chosen[jax.random.permutation(key_rows, rows)]
        within = jax.random.randint(key_face, (rows,), 0, block_faces)
        return (dest_dev[chosen], face_block[chosen] * block_faces + within)
    targets, places = jax.vmap(per_source)(jnp.arange(DEVICES, dtype=jnp.int32))
    return (targets.reshape(-1).astype(jnp.int32), places.reshape(-1).astype(jnp.int32))


def draw_slave_dest(key, part):
    targets, places = pair_layout(jax.random.fold_in(key, 101), S_DEV, SLOT_CAP)
    return targets[:, None]


def draw_face_slot(key, part):
    targets, places = pair_layout(jax.random.fold_in(key, 101), S_DEV, SLOT_CAP)
    return places


def draw_mirror_dest(key, part):
    targets, places = pair_layout(jax.random.fold_in(key, 202), M_DEV, MIRROR_CAP)
    return targets[:, None]


def draw_mirror_slot(key, part):
    targets, places = pair_layout(jax.random.fold_in(key, 202), M_DEV, MIRROR_CAP)
    return places


def with_ends(entries, key, least, high):
    longest = entries.shape.index(max(entries.shape))
    spots = []
    for shift in (0, 1):
        where = [jax.random.randint(jax.random.fold_in(key, axis), (), 0, length) for axis, length in enumerate(entries.shape)]
        where[longest] = (where[longest] + shift) % entries.shape[longest]
        spots.append(tuple(where))
    return entries.at[spots[0]].set(least).at[spots[1]].set(high)


def levels(key, shape, pieces, least, high):
    def one(position, shards_of):
        heights = jax.random.uniform(jax.random.fold_in(jax.random.fold_in(key, 6), position), (shards_of,), jnp.float32, least / len(pieces), high / len(pieces))
        return jnp.repeat(jnp.exp(heights), shape[position] // shards_of).reshape((-1,) + (1,) * (len(shape) - position - 1))

    gain = one(*pieces[0])
    for cut in pieces[1:]:
        gain = gain * one(*cut)
    return gain


def setup_inputs(seed: int = 0) -> dict:
    key_list = jax.random.split(jax.random.key(seed), 12)
    face_coords = draw_face_coords(jax.random.fold_in(key_list[11], 71), 0)
    face_stiff = jnp.clip(jnp.exp(math.log(10.0) - 2.3025851 * jax.random.uniform(key_list[1], (FACES,), jnp.float32) ** levels(key_list[1], (FACES,), ((0, 128),), -0.2, 0.2)), 1.0, 10.0)
    bin_order = jax.vmap(lambda own: jax.random.permutation(own, F_DEV))(jax.random.split(key_list[2], DEVICES)).reshape((DEVICES, F_DEV)).astype(jnp.int32)
    slave_pos = draw_slave_pos(jax.random.fold_in(key_list[11], 71), 0)
    slave_dest = draw_slave_dest(jax.random.fold_in(key_list[11], 71), 0)
    face_slot = draw_face_slot(jax.random.fold_in(key_list[11], 71), 0)
    block_count = with_ends(jax.random.randint(key_list[6], (DEVICES, S_DEV // 128), 64, 129), jax.random.fold_in(key_list[6], 1), 64, 128).astype(jnp.int32)
    mirror_face = with_ends(jax.random.randint(key_list[7], (MIRRORS,), 0, F_DEV), jax.random.fold_in(key_list[7], 1), 0, F_DEV - 1).astype(jnp.int32)
    mirror_node = with_ends(jax.random.randint(key_list[8], (MIRRORS,), 0, 9), jax.random.fold_in(key_list[8], 1), 0, 8).astype(jnp.int32)
    mirror_dest = draw_mirror_dest(jax.random.fold_in(key_list[11], 71), 0)
    mirror_slot = draw_mirror_slot(jax.random.fold_in(key_list[11], 71), 0)
    return dict(face_coords=face_coords, face_stiff=face_stiff, bin_order=bin_order, slave_pos=slave_pos, slave_dest=slave_dest, face_slot=face_slot, block_count=block_count, mirror_face=mirror_face, mirror_node=mirror_node, mirror_dest=mirror_dest, mirror_slot=mirror_slot)


CLIP_EDGE = 1.1

def lagrange(coord):
    values = (coord * (coord - 1.0) * 0.5, 1.0 - coord * coord, coord * (coord + 1.0) * 0.5)
    slopes = (coord - 0.5, -2.0 * coord, coord + 0.5)
    return (values, slopes)

def shape_table(local_u, local_v):
    val_u, slope_u = lagrange(local_u)
    val_v, slope_v = lagrange(local_v)
    weights = jnp.stack([val_u[i] * val_v[j] for j in range(3) for i in range(3)])
    deriv_u = jnp.stack([slope_u[i] * val_v[j] for j in range(3) for i in range(3)])
    deriv_v = jnp.stack([val_u[i] * slope_v[j] for j in range(3) for i in range(3)])
    return (weights, deriv_u, deriv_v)

def surface_terms(nodes, local_u, local_v):
    weights, deriv_u, deriv_v = shape_table(local_u, local_v)
    surface = lax.optimization_barrier(jnp.sum(weights[:, None, :] * nodes, 0))
    tangent_u = lax.optimization_barrier(jnp.sum(deriv_u[:, None, :] * nodes, 0))
    tangent_v = lax.optimization_barrier(jnp.sum(deriv_v[:, None, :] * nodes, 0))
    return (weights, surface, tangent_u, tangent_v)

def project(points, face_nodes, stiffness, weight):
    count = points.shape[1]
    nodes = face_nodes.reshape(9, 3, count)
    local_u = jnp.zeros((count,), jnp.float32)
    local_v = jnp.zeros((count,), jnp.float32)
    for newton_step in range(NEWTON):
        weights, surface, tangent_u, tangent_v = surface_terms(nodes, local_u, local_v)
        offset = points - surface
        a_uu = lax.optimization_barrier(jnp.sum(tangent_u * tangent_u, 0))
        a_uv = lax.optimization_barrier(jnp.sum(tangent_u * tangent_v, 0))
        a_vv = lax.optimization_barrier(jnp.sum(tangent_v * tangent_v, 0))
        b_u = lax.optimization_barrier(jnp.sum(tangent_u * offset, 0))
        b_v = lax.optimization_barrier(jnp.sum(tangent_v * offset, 0))
        determinant = a_uu * a_vv - a_uv * a_uv
        local_u = jnp.clip(local_u + (a_vv * b_u - a_uv * b_v) / determinant, -CLIP_EDGE, CLIP_EDGE)
        local_v = jnp.clip(local_v + (a_uu * b_v - a_uv * b_u) / determinant, -CLIP_EDGE, CLIP_EDGE)
    weights, surface, tangent_u, tangent_v = surface_terms(nodes, local_u, local_v)
    normal = jnp.stack([tangent_u[1] * tangent_v[2] - tangent_u[2] * tangent_v[1], tangent_u[2] * tangent_v[0] - tangent_u[0] * tangent_v[2], tangent_u[0] * tangent_v[1] - tangent_u[1] * tangent_v[0]])
    normal = normal / jnp.sqrt(lax.optimization_barrier(jnp.sum(normal * normal, 0)))
    penetration = jnp.maximum(-lax.optimization_barrier(jnp.sum((points - surface) * normal, 0)), 0.0)
    contact_force = (0.5 * stiffness * weight * penetration)[None, :] * normal
    reaction = -(weights[:, None, :] * contact_force[None, :, :]).reshape(27, count)
    return (contact_force, reaction)

def reference(face_coords, face_stiff, bin_order, slave_pos, slave_dest, face_slot, block_count, mirror_face, mirror_node, mirror_dest, mirror_slot):
    devices = N_MECH * N_BIN
    block_faces = F_DEV // N_BIN

    def target(dest_dev, slot_index):
        mech_row = dest_dev // N_BIN
        bin_col = dest_dev % N_BIN
        peer = slot_index // block_faces
        within = slot_index % block_faces
        owner = (mech_row * N_BIN + peer).astype(jnp.int32)
        local = bin_order[owner, (bin_col * block_faces + within).astype(jnp.int32)]
        return (owner * F_DEV + local).astype(jnp.int32)

    def visit(carry, inputs):
        owner, points, dests, slots, counts, mfaces, mnodes, mdests, mslots = inputs
        positions = jnp.arange(S_DEV, dtype=jnp.int32)
        live_mask = (positions % 128 < jnp.repeat(counts, 128)).astype(jnp.float32)
        gface = target(dests, slots)
        contact_force, reaction = project(points, face_coords[:, gface], face_stiff[gface], live_mask)
        carry = carry.at[:, gface].add(reaction)
        source = (owner * F_DEV + mfaces).astype(jnp.int32)
        node_rows = (3 * mnodes[None, :] + jnp.arange(3, dtype=jnp.int32)[:, None]).astype(jnp.int32)
        mirror_points = face_coords[node_rows, source[None, :]]
        mface_global = target(mdests, mslots)
        mirror_force, mirror_reaction = project(mirror_points, face_coords[:, mface_global], face_stiff[mface_global], jnp.ones((M_DEV,), jnp.float32))
        carry = carry.at[:, mface_global].add(mirror_reaction)
        carry = carry.at[node_rows, source[None, :]].add(mirror_force)
        return (carry, contact_force)
    inputs = (jnp.arange(devices, dtype=jnp.int32), slave_pos.reshape(3, devices, S_DEV).transpose(1, 0, 2), slave_dest[:, 0].reshape(devices, S_DEV), face_slot.reshape(devices, S_DEV), block_count, mirror_face.reshape(devices, M_DEV), mirror_node.reshape(devices, M_DEV), mirror_dest[:, 0].reshape(devices, M_DEV), mirror_slot.reshape(devices, M_DEV))
    start = jnp.zeros((27, F_DEV * devices), jnp.float32)
    face_force, forces = lax.scan(visit, start, inputs)
    slave_force = forces.transpose(1, 0, 2).reshape(3, S_DEV * devices)
    return (slave_force, face_force)
```

```python
import functools

import jax
import jax.numpy as jnp
from jax import lax
from jax.experimental import pallas as pl
from jax.experimental.pallas import tpu as pltpu
from jax.sharding import PartitionSpec as P

NEWTON = 5
CLIP_EDGE = 1.1
F32 = jnp.float32
BF16 = jnp.bfloat16
I32 = jnp.int32
LANES = 128
SB = 32
MB = 16
FT = 16
DEV = 128
NBIN = 8
SK = 64
MK = 32


def iota(shape, dim):
    return lax.broadcasted_iota(I32, shape, dim)


def dot_nt(a, b):
    return lax.dot_general(a, b, (((1,), (1,)), ((), ())), preferred_element_type=F32)


def row_gather(row, lane, shape):
    return jnp.take_along_axis(jnp.broadcast_to(row, shape), lane, axis=1)


def call(body, out_shape, scratch=(), in_specs=None, cost=0):
    kwargs = {} if in_specs is None else {"in_specs": in_specs}
    return pl.pallas_call(
        body,
        out_shape=out_shape,
        scratch_shapes=list(scratch),
        cost_estimate=pl.CostEstimate(flops=cost, bytes_accessed=cost // 100, transcendentals=0),
        **kwargs,
    )


VM = pl.BlockSpec(memory_space=pltpu.VMEM)
SM = pl.BlockSpec(memory_space=pltpu.SMEM)


def pack_body(
    count_ref, sdest_ref, sslot_ref, spos_ref, mdest_ref, mslot_ref, mface_ref, mnode_ref, coords_ref,
    send_ref, speer_ref, sk_ref, mpeer_ref, mk_ref,
    cell_ref, e_ref, b_ref, code_ref, cols_ref, hot_ref, val_ref, mval_ref, cnt_ref, pts_ref, rows_ref,
):
    def keys(dest, slot):
        owner = (dest & ~(NBIN - 1)) | (slot >> 8)
        return owner, dest & (NBIN - 1), (slot & 255) + 1

    owner, col, code = keys(sdest_ref[...], sslot_ref[...])
    e_ref[0:SB] = owner
    b_ref[0:SB] = col
    code_ref[0:SB] = code.astype(F32)
    speer_ref[...] = owner
    cell_ref[0:SB] = (owner * NBIN + col).astype(F32)
    owner, col, code = keys(mdest_ref[...], mslot_ref[...])
    e_ref[SB:SB + MB] = owner
    b_ref[SB:SB + MB] = col
    code_ref[SB:SB + MB] = code.astype(F32)
    mpeer_ref[...] = owner
    cell_ref[SB:SB + MB] = (owner * NBIN + col).astype(F32)
    cell_ref[SB + MB:] = jnp.zeros((LANES - SB - MB, LANES), F32)
    cols_ref[...] = cell_ref[...].T

    sub = iota((LANES, LANES), 0)
    lane_row = iota((1, LANES), 1)
    earlier = sub < iota((LANES, LANES), 1)
    sub8 = iota((NBIN, LANES), 0)
    sub16 = iota((16, LANES), 0)

    for r in range(SB + MB):
        hot = jnp.where(sub == e_ref[r:r + 1, :], 1.0, 0.0).astype(BF16)
        hot_ref[:, r * LANES:(r + 1) * LANES] = hot
        bins = jnp.where(sub16 == b_ref[r:r + 1, :], 1.0, 0.0).astype(BF16)
        cnt_ref[r] = dot_nt(bins, hot)[:NBIN]

    for first, last, cap, rows, vals, kout in (
        (0, SB, 8, SK, val_ref, sk_ref),
        (SB, SB + MB, 4, MK, mval_ref, mk_ref),
    ):
        seen = jnp.zeros((NBIN, LANES), F32)
        slot_iota = iota((rows, LANES), 0)
        for r in range(first, last):
            i = r - first
            peers = jnp.broadcast_to(e_ref[r:r + 1, :], (NBIN, LANES))
            before = jnp.where(
                sub8 == b_ref[r:r + 1, :], jnp.take_along_axis(seen, peers, axis=1), 0.0
            )
            same = cell_ref[r:r + 1, :] == cols_ref[:, r:r + 1]
            inside = jnp.where(same & earlier, 1.0, 0.0)
            rank = jnp.sum(inside, 0, keepdims=True) + jnp.sum(before, 0, keepdims=True)
            k = b_ref[r:r + 1, :] * cap + rank.astype(I32)
            if first == 0:
                k = jnp.where(lane_row < count_ref[0, i], k, -1)
            kout[i:i + 1, :] = k
            mine = slot_iota == k
            vals[0:rows, i * LANES:(i + 1) * LANES] = jnp.where(mine, float(i + 1), 0.0).astype(BF16)
            vals[rows:2 * rows, i * LANES:(i + 1) * LANES] = jnp.where(
                mine, lane_row.astype(F32), 0.0
            ).astype(BF16)
            seen = seen + cnt_ref[r]

    face = mface_ref[...]
    tile = face >> 7
    lane = face & 127
    node = mnode_ref[...]
    for c in range(3):
        point = jnp.zeros((MB, LANES), F32)
        for n in range(9):
            part = jnp.zeros((MB, LANES), F32)
            for t in range(FT):
                got = row_gather(
                    coords_ref[3 * n + c:3 * n + c + 1, t * LANES:(t + 1) * LANES], lane, (MB, LANES)
                )
                part = jnp.where(tile == t, got, part)
            point = jnp.where(node == n, part, point)
        pts_ref[c] = point

    sinv = dot_nt(val_ref[...], hot_ref[:, 0:SB * LANES])
    source = sinv[0:SK].astype(I32) - 1
    lane = sinv[SK:2 * SK].astype(I32)
    for c in range(4):
        out = jnp.zeros((SK, LANES), F32)
        for r in range(SB):
            if c < 3:
                row = spos_ref[c:c + 1, r * LANES:(r + 1) * LANES]
            else:
                row = code_ref[r:r + 1, :]
            out = jnp.where(source == r, row_gather(row, lane, (SK, LANES)), out)
        rows_ref[c * SK:(c + 1) * SK] = out
    minv = dot_nt(mval_ref[...], hot_ref[:, SB * LANES:])
    source = minv[0:MK].astype(I32) - 1
    lane = minv[MK:2 * MK].astype(I32)
    for c in range(4):
        out = jnp.zeros((MK, LANES), F32)
        for r in range(MB):
            if c < 3:
                row = pts_ref[c, r:r + 1, :]
            else:
                row = code_ref[SB + r:SB + r + 1, :]
            out = jnp.where(source == r, row_gather(row, lane, (MK, LANES)), out)
        rows_ref[4 * SK + c * MK:4 * SK + (c + 1) * MK] = out
    for i in range(3):
        send_ref[pl.ds(i, DEV, stride=3), :] = rows_ref[i * LANES:(i + 1) * LANES].T


def pack(count, sdest, sslot, spos, mdest, mslot, mface, mnode, coords):
    blocks = SB + MB
    return call(
        pack_body,
        (
            jax.ShapeDtypeStruct((3 * DEV, LANES), F32),
            jax.ShapeDtypeStruct((SB, LANES), I32),
            jax.ShapeDtypeStruct((SB, LANES), I32),
            jax.ShapeDtypeStruct((MB, LANES), I32),
            jax.ShapeDtypeStruct((MB, LANES), I32),
        ),
        [
            pltpu.VMEM((LANES, LANES), F32),
            pltpu.VMEM((blocks, LANES), I32),
            pltpu.VMEM((blocks, LANES), I32),
            pltpu.VMEM((blocks, LANES), F32),
            pltpu.VMEM((LANES, LANES), F32),
            pltpu.VMEM((LANES, blocks * LANES), BF16),
            pltpu.VMEM((2 * SK, SB * LANES), BF16),
            pltpu.VMEM((2 * MK, MB * LANES), BF16),
            pltpu.VMEM((blocks, NBIN, LANES), F32),
            pltpu.VMEM((3, MB, LANES), F32),
            pltpu.VMEM((3 * LANES, LANES), F32),
        ],
        in_specs=[SM] + [VM] * 8,
        cost=10**9,
    )(count, sdest, sslot, spos, mdest, mslot, mface, mnode, coords)


def order_body(coords_ref, stiff_ref, order_ref, mface_ref, table_ref, inv_ref, mhot_ref, hot_ref, val_ref, src_ref):
    src_ref[0:27] = coords_ref[...]
    src_ref[27:28] = stiff_ref[...]
    src_ref[28:32] = jnp.zeros((4, FT * LANES), F32)
    sub = iota((LANES, LANES), 0)
    sub16 = iota((FT, LANES), 0)
    lane_row = iota((1, LANES), 1).astype(F32)
    for m in range(FT):
        order = order_ref[m:m + 1, :]
        hi = order >> 7
        lo = order & 127
        lane = jnp.broadcast_to(lo, (32, LANES))
        out = jnp.zeros((32, LANES), F32)
        for t in range(FT):
            got = jnp.take_along_axis(src_ref[:, t * LANES:(t + 1) * LANES], lane, axis=1)
            out = jnp.where(hi == t, got, out)
        table_ref[:, m * LANES:(m + 1) * LANES] = out
        hot_ref[:, m * LANES:(m + 1) * LANES] = jnp.where(sub == lo, 1.0, 0.0).astype(BF16)
        mine = sub16 == hi
        val_ref[0:FT, m * LANES:(m + 1) * LANES] = jnp.where(mine, float(m), 0.0).astype(BF16)
        val_ref[FT:2 * FT, m * LANES:(m + 1) * LANES] = jnp.where(mine, lane_row, 0.0).astype(BF16)
    inv_ref[...] = dot_nt(val_ref[...], hot_ref[...]).astype(I32)
    big = iota((FT * LANES, LANES), 0)
    for r in range(MB):
        mhot_ref[:, r * LANES:(r + 1) * LANES] = jnp.where(
            big == mface_ref[r:r + 1, :], 1.0, 0.0
        ).astype(BF16)


def order_faces(coords, stiff, order, mface):
    faces = FT * LANES
    return call(
        order_body,
        (
            jax.ShapeDtypeStruct((32, faces), F32),
            jax.ShapeDtypeStruct((2 * FT, LANES), I32),
            jax.ShapeDtypeStruct((faces, MB * LANES), BF16),
        ),
        [
            pltpu.VMEM((LANES, faces), BF16),
            pltpu.VMEM((2 * FT, faces), BF16),
            pltpu.VMEM((32, faces), F32),
        ],
        cost=10**9,
    )(coords, stiff, order, mface)


def quadratic(low, mid, high):
    return mid, 0.5 * (high - low), 0.5 * (high + low) - mid


def project(point, nodes, stiff):
    coef = []
    for c in range(3):
        by_j = [quadratic(nodes[3 * j][c], nodes[3 * j + 1][c], nodes[3 * j + 2][c]) for j in range(3)]
        coef.append([quadratic(by_j[0][p], by_j[1][p], by_j[2][p]) for p in range(3)])

    def surface(u, v):
        u2 = u + u
        v2 = v + v
        x, tu, tv = [], [], []
        for c in range(3):
            k = coef[c]
            h = [k[0][q] + u * (k[1][q] + u * k[2][q]) for q in range(3)]
            d = [k[1][q] + u2 * k[2][q] for q in range(3)]
            x.append(h[0] + v * (h[1] + v * h[2]))
            tu.append(d[0] + v * (d[1] + v * d[2]))
            tv.append(h[1] + v2 * h[2])
        return x, tu, tv

    def inner(a, b):
        return a[0] * b[0] + a[1] * b[1] + a[2] * b[2]

    u = v = jnp.zeros_like(point[0])
    for step in range(NEWTON):
        if step == 0:
            x = [coef[c][0][0] for c in range(3)]
            tu = [coef[c][1][0] for c in range(3)]
            tv = [coef[c][0][1] for c in range(3)]
        else:
            x, tu, tv = surface(u, v)
        o = [point[c] - x[c] for c in range(3)]
        a_uu, a_uv, a_vv = inner(tu, tu), inner(tu, tv), inner(tv, tv)
        b_u, b_v = inner(tu, o), inner(tv, o)
        scale = 1.0 / (a_uu * a_vv - a_uv * a_uv)
        du = (a_vv * b_u - a_uv * b_v) * scale
        dv = (a_uu * b_v - a_uv * b_u) * scale
        u = jnp.clip(u + du, -CLIP_EDGE, CLIP_EDGE)
        v = jnp.clip(v + dv, -CLIP_EDGE, CLIP_EDGE)
    x, tu, tv = surface(u, v)
    n = [
        tu[1] * tv[2] - tu[2] * tv[1],
        tu[2] * tv[0] - tu[0] * tv[2],
        tu[0] * tv[1] - tu[1] * tv[0],
    ]
    unit = 1.0 / jnp.sqrt(inner(n, n))
    gap = inner([point[c] - x[c] for c in range(3)], n) * unit
    size = 0.5 * stiff * jnp.maximum(-gap, 0.0) * unit
    return u, v, [size * n[c] for c in range(3)]


def force_body(recv_ref, table_ref, back_ref, uv_ref, force_ref, index_ref, rows_ref):
    for i in range(3):
        rows_ref[i * LANES:(i + 1) * LANES] = recv_ref[pl.ds(i, DEV, stride=3), :].T
    shape = (8, LANES)
    upper = iota(shape, 0) < 4
    force_ref[3 * SK + 3 * MK:] = jnp.zeros((LANES - 32, LANES), F32)
    for g in range(12):
        if g < 8:
            at = [c * SK + g * 8 for c in range(4)]
            out = [c * SK + g * 8 for c in range(3)]
        else:
            at = [4 * SK + c * MK + (g - 8) * 8 for c in range(4)]
            out = [3 * SK + c * MK + (g - 8) * 8 for c in range(3)]
        point = [rows_ref[at[c]:at[c] + 8, :] for c in range(3)]
        code = rows_ref[at[3]:at[3] + 8, :].astype(I32)
        index = jnp.maximum(code - 1, 0)
        lane = index & 127
        high = index >= LANES

        def entry(row, half):
            def tile(t):
                return jnp.broadcast_to(table_ref[row:row + 1, t * LANES:(t + 1) * LANES], shape)

            if g < 8:
                return tile(2 * g + half)
            first = 4 * (g - 8)
            return jnp.where(upper, tile(first + half), tile(first + 2 + half))

        def pick(row):
            got = [jnp.take_along_axis(entry(row, half), lane, axis=1) for half in range(2)]
            return jnp.where(high, got[1], got[0])

        nodes = [[pick(3 * a + c) for c in range(3)] for a in range(9)]
        stiff = jnp.where(code > 0, pick(27), 0.0)
        u, v, force = project(point, nodes, stiff)
        uv_ref[g * 8:g * 8 + 8] = u
        uv_ref[96 + g * 8:96 + g * 8 + 8] = v
        index_ref[g * 8:g * 8 + 8] = index
        for c in range(3):
            force_ref[out[c]:out[c] + 8] = force[c]
    for i in range(3):
        back_ref[pl.ds(i, DEV, stride=3), :] = force_ref[i * LANES:(i + 1) * LANES].T


def forces(recv, table):
    return call(
        force_body,
        (
            jax.ShapeDtypeStruct((3 * DEV, LANES), F32),
            jax.ShapeDtypeStruct((192, LANES), F32),
            jax.ShapeDtypeStruct((3 * LANES, LANES), F32),
            jax.ShapeDtypeStruct((96, LANES), I32),
        ),
        [pltpu.VMEM((3 * LANES, LANES), F32)],
        cost=10**9,
    )(recv, table)


def split(x):
    high = x.astype(BF16)
    return high, (x - high.astype(F32)).astype(BF16)


def react_body(uv_ref, force_ref, index_ref, inv_ref, out_ref, part_ref, lhs_ref, hot_ref, sum_ref):
    part_ref[27 * 8:] = jnp.zeros((40, LANES), F32)
    sub = iota((2 * LANES, LANES), 0)

    def fill(g, first, count, at):
        for k in range(count):
            rows = part_ref[pl.ds(first + k, 32, stride=8), :]
            high, low = split(rows)
            lhs_ref[0:32, (at + k) * LANES:(at + k + 1) * LANES] = high
            lhs_ref[32:64, (at + k) * LANES:(at + k + 1) * LANES] = low
            row = g * 8 + first + k
            hot_ref[:, (at + k) * LANES:(at + k + 1) * LANES] = jnp.where(
                sub == index_ref[row:row + 1, :], 1.0, 0.0
            ).astype(BF16)

    def reactions(g):
        u = uv_ref[g * 8:g * 8 + 8]
        v = uv_ref[96 + g * 8:96 + g * 8 + 8]
        lu = (u * (u - 1.0) * 0.5, 1.0 - u * u, u * (u + 1.0) * 0.5)
        lv = (v * (v - 1.0) * 0.5, 1.0 - v * v, v * (v + 1.0) * 0.5)
        for c in range(3):
            row = c * SK + g * 8 if g < 8 else 3 * SK + c * MK + (g - 8) * 8
            f = -force_ref[row:row + 8]
            for j in range(3):
                fj = f * lv[j]
                for i in range(3):
                    a = 3 * (i + 3 * j) + c
                    part_ref[a * 8:a * 8 + 8] = lu[i] * fj

    for b in range(NBIN):
        reactions(b)
        fill(b, 0, 8, 0)
        reactions(8 + b // 2)
        fill(8 + b // 2, 4 * (b % 2), 4, 8)
        both = dot_nt(lhs_ref[...], hot_ref[...])
        sum_ref[:, b * 256:(b + 1) * 256] = both[0:32] + both[32:64]

    for m in range(FT):
        hi = inv_ref[m:m + 1, :]
        lane = jnp.broadcast_to(inv_ref[FT + m:FT + m + 1, :], (32, LANES))
        out = jnp.zeros((32, LANES), F32)
        for t in range(FT):
            got = jnp.take_along_axis(sum_ref[:, t * LANES:(t + 1) * LANES], lane, axis=1)
            out = jnp.where(hi == t, got, out)
        out_ref[:, m * LANES:(m + 1) * LANES] = out


def react(uv, force, index, inv):
    return call(
        react_body,
        jax.ShapeDtypeStruct((32, FT * LANES), F32),
        [
            pltpu.VMEM((256, LANES), F32),
            pltpu.VMEM((64, 12 * LANES), BF16),
            pltpu.VMEM((256, 12 * LANES), BF16),
            pltpu.VMEM((32, FT * LANES), F32),
        ],
        cost=10**9,
    )(uv, force, index, inv)


def finish_body(
    back_ref, speer_ref, sk_ref, mpeer_ref, mk_ref, mnode_ref, mhot_ref, part_ref,
    slave_ref, face_ref, rows_ref, own_ref, lhs_ref,
):
    for i in range(3):
        rows_ref[i * LANES:(i + 1) * LANES] = back_ref[pl.ds(i, DEV, stride=3), :].T
    peer = mpeer_ref[...]
    slot = mk_ref[...]
    for c in range(3):
        out = jnp.zeros((MB, LANES), F32)
        for k in range(MK):
            row = 3 * SK + c * MK + k
            out = jnp.where(slot == k, row_gather(rows_ref[row:row + 1, :], peer, (MB, LANES)), out)
        own_ref[c] = out
    sub = iota((32, LANES), 0)
    comp = sub % 3
    node = sub // 3
    for r in range(MB):
        f = jnp.where(comp == 0, own_ref[0, r:r + 1, :], own_ref[1, r:r + 1, :])
        f = jnp.where(comp == 2, own_ref[2, r:r + 1, :], f)
        f = jnp.where(node == mnode_ref[r:r + 1, :], f, 0.0)
        high, low = split(f)
        lhs_ref[0:32, r * LANES:(r + 1) * LANES] = high
        lhs_ref[32:64, r * LANES:(r + 1) * LANES] = low
    both = dot_nt(lhs_ref[...], mhot_ref[...])
    face_ref[...] = (part_ref[...] + both[0:32] + both[32:64])[0:27]

    peer = speer_ref[...]
    slot = sk_ref[...]
    for c in range(3):
        out = jnp.zeros((SB, LANES), F32)
        for k in range(SK):
            row = c * SK + k
            out = jnp.where(slot == k, row_gather(rows_ref[row:row + 1, :], peer, (SB, LANES)), out)
        for r in range(SB):
            slave_ref[c:c + 1, r * LANES:(r + 1) * LANES] = out[r:r + 1, :]


def finish(back, speer, sk, mpeer, mk, mnode, mhot, part):
    return call(
        finish_body,
        (
            jax.ShapeDtypeStruct((3, SB * LANES), F32),
            jax.ShapeDtypeStruct((27, FT * LANES), F32),
        ),
        [
            pltpu.VMEM((3 * LANES, LANES), F32),
            pltpu.VMEM((3, MB, LANES), F32),
            pltpu.VMEM((64, MB * LANES), BF16),
        ],
        cost=10**9,
    )(back, speer, sk, mpeer, mk, mnode, mhot, part)


def exchange(x):
    x = x.reshape(DEV, 1, 3 * LANES)
    x = lax.all_to_all(x, ("mech", "bin"), split_axis=0, concat_axis=0, tiled=True)
    return x.reshape(3 * DEV, LANES)


def shards(
    face_coords, face_stiff, bin_order, slave_pos, slave_dest, face_slot, block_count,
    mirror_face, mirror_node, mirror_dest, mirror_slot,
):
    mface = mirror_face.reshape(MB, LANES)
    mnode = mirror_node.reshape(MB, LANES)
    send, speer, sk, mpeer, mk = pack(
        block_count,
        slave_dest.reshape(SB, LANES),
        face_slot.reshape(SB, LANES),
        slave_pos,
        mirror_dest.reshape(MB, LANES),
        mirror_slot.reshape(MB, LANES),
        mface,
        mnode,
        face_coords,
    )
    recv = exchange(send)
    table, inv, mhot = order_faces(
        face_coords, face_stiff.reshape(1, FT * LANES), bin_order.reshape(FT, LANES), mface
    )
    back, uv, force, index = forces(recv, table)
    returned = exchange(back)
    part = react(uv, force, index, inv)
    return finish(returned, speer, sk, mpeer, mk, mnode, mhot, part)


def solution(mesh):
    axes = ("mech", "bin")
    return jax.shard_map(
        shards,
        mesh=mesh,
        in_specs=(
            P(None, axes), P(axes), P(axes, None), P(None, axes), P(axes, None), P(axes),
            P(axes, None), P(axes), P(axes), P(axes, None), P(axes),
        ),
        out_specs=(P(None, axes), P(None, axes)),
        check_vma=False,
    )
```

```python
import functools

import jax
import jax.numpy as jnp
from jax import lax
from jax.experimental import pallas as pl
from jax.experimental.pallas import tpu as pltpu
from jax.sharding import PartitionSpec as P

NEWTON = 5
CLIP_EDGE = 1.1
VMEM_BYTES = 16 * 2**20
F32 = jnp.float32
BF16 = jnp.bfloat16
I32 = jnp.int32
I16 = jnp.int16
LANES = 128
SB = 32
MB = 16
FT = 16
DEV = 128
NBIN = 8
SK = 64
MK = 32


def iota(shape, dim):
    return lax.broadcasted_iota(I32, shape, dim)


def dot_nt(a, b):
    return lax.dot_general(a, b, (((1,), (1,)), ((), ())), preferred_element_type=F32)


def wide16(row, rows):
    narrow = jnp.broadcast_to(row, (16, LANES)).astype(I16)
    return jnp.concatenate([narrow] * (rows // 16), 0) if rows > 16 else narrow


def slot_rows(rows):
    return iota((rows, LANES), 0).astype(I16)


def pick_bf16(rows16, row):
    hit = rows16 == wide16(row, rows16.shape[0])
    return jnp.where(hit, jnp.ones(rows16.shape, BF16), jnp.zeros(rows16.shape, BF16))


def one_hot(rows, row):
    return pick_bf16(slot_rows(rows), row)


def row_gather(row, lane, shape):
    return jnp.take_along_axis(jnp.broadcast_to(row, shape), lane, axis=1)


def call(body, out_shape, scratch=(), in_specs=None, cost=0):
    kwargs = {} if in_specs is None else {"in_specs": in_specs}
    return pl.pallas_call(
        body,
        out_shape=out_shape,
        scratch_shapes=list(scratch),
        compiler_params=pltpu.CompilerParams(vmem_limit_bytes=VMEM_BYTES),
        cost_estimate=pl.CostEstimate(flops=cost, bytes_accessed=cost // 100, transcendentals=0),
        **kwargs,
    )


VM = pl.BlockSpec(memory_space=pltpu.VMEM)
SM = pl.BlockSpec(memory_space=pltpu.SMEM)


def pack_body(
    count_ref, sdest_ref, sslot_ref, spos_ref, mdest_ref, mslot_ref, mface_ref, mnode_ref, coords_ref,
    send_ref, speer_ref, sk_ref, mpeer_ref, mk_ref,
    cell_ref, e_ref, b_ref, code_ref, turn_ref, cols_ref, cnt_ref, pts_ref, rows_ref,
):
    def keys(dest, slot):
        owner = (dest & ~(NBIN - 1)) | (slot >> 8)
        return owner, dest & (NBIN - 1), (slot & 255) + 1

    half = LANES // 2
    for first, rows, dest_ref, slot_ref, peer_ref in (
        (0, SB, sdest_ref, sslot_ref, speer_ref),
        (SB, MB, mdest_ref, mslot_ref, mpeer_ref),
    ):
        owner, col, code = keys(dest_ref[...], slot_ref[...])
        e_ref[first:first + rows] = owner
        b_ref[first:first + rows] = col
        code_ref[first:first + rows] = code.astype(F32)
        peer_ref[...] = owner
        cell = (owner * NBIN + col).astype(F32)
        cell_ref[first:first + rows] = cell
        turn_ref[first:first + rows] = cell
        turn_ref[half + first:half + first + rows] = pltpu.roll(cell, half, axis=1)
    for first in (SB + MB, half + SB + MB):
        turn_ref[first:first + half - SB - MB] = jnp.zeros((half - SB - MB, LANES), F32)
    cols_ref[...] = turn_ref[...].T

    lane_row = iota((1, LANES), 1)
    lane8 = iota((NBIN, LANES), 1)
    earlier = iota((half, LANES), 0) < (iota((half, LANES), 1) & (half - 1))
    sub8 = iota((NBIN, LANES), 0)
    upper = lane8 >= half
    row16 = iota((16, LANES), 0)
    bin_rows = jnp.where((row16 < 8) | (iota((16, LANES), 1) < half), row16 & 7, -1).astype(I16)
    lanes_bf = iota((64, LANES), 1).astype(F32).astype(BF16)

    for r in range(SB + MB):
        bins = pick_bf16(bin_rows, b_ref[r:r + 1, :])
        cnt_ref[r] = dot_nt(bins, one_hot(LANES, e_ref[r:r + 1, :]))

    def slots(first, last, cap, rows, kout):
        seen = jnp.zeros((NBIN, LANES), F32)
        inverse = jnp.zeros((2 * rows, LANES), F32)
        for group in range(first, last, 4):
            left, right = [], []
            for r in range(group, group + 4):
                i = r - first
                peers = jnp.broadcast_to(e_ref[r:r + 1, :], (NBIN, LANES))
                column = jnp.where(upper, half + r, r)
                before = jnp.take_along_axis(seen, peers, axis=1) + jnp.where(
                    upper, jnp.take_along_axis(cnt_ref[r, 8:16], peers, axis=1), 0.0
                )
                before = jnp.where(sub8 == b_ref[r:r + 1, :], before, 0.0)
                for m in range(half // 8):
                    col = jnp.take_along_axis(cols_ref[8 * m:8 * m + 8], column, axis=1)
                    same = (cell_ref[r:r + 1, :] == col) & earlier[8 * m:8 * m + 8]
                    before = before + jnp.where(same, 1.0, 0.0)
                rank = jnp.sum(before, 0, keepdims=True)
                k = b_ref[r:r + 1, :] * cap + rank.astype(I32)
                if first == 0:
                    k = jnp.where(lane_row < count_ref[0, i], k, -1)
                kout[i:i + 1, :] = k
                mine = slot_rows(rows) == wide16(k, rows)
                left.append(jnp.concatenate([
                    jnp.where(mine, jnp.full((rows, LANES), i + 1, BF16), jnp.zeros((rows, LANES), BF16)),
                    jnp.where(mine, lanes_bf[:rows], jnp.zeros((rows, LANES), BF16)),
                ], 0))
                right.append(one_hot(LANES, e_ref[r:r + 1, :]))
                seen = seen + cnt_ref[r, 0:8]
            inverse = inverse + dot_nt(jnp.concatenate(left, 1), jnp.concatenate(right, 1))
        return inverse

    sinv = slots(0, SB, 8, SK, sk_ref)
    minv = slots(SB, SB + MB, 4, MK, mk_ref)

    for m in range(MB // 8):
        face = mface_ref[8 * m:8 * m + 8]
        tile = face >> 7
        lane = face & 127
        node = mnode_ref[8 * m:8 * m + 8]
        at_tile = [tile == t for t in range(FT)]
        for c in range(3):
            point = jnp.zeros((8, LANES), F32)
            for n in range(9):
                part = jnp.zeros((8, LANES), F32)
                for t in range(FT):
                    got = row_gather(
                        coords_ref[3 * n + c:3 * n + c + 1, t * LANES:(t + 1) * LANES], lane, (8, LANES)
                    )
                    part = jnp.where(at_tile[t], got, part)
                point = jnp.where(node == n, part, point)
            pts_ref[c, 8 * m:8 * m + 8] = point

    for blocks, rows, inverse, base in ((SB, SK, sinv, 0), (MB, MK, minv, 4 * SK)):
        for m in range(rows // 8):
            source = inverse[8 * m:8 * m + 8].astype(I32) - 1
            lane = inverse[rows + 8 * m:rows + 8 * m + 8].astype(I32)
            at_block = [source == r for r in range(blocks)]
            for c in range(4):
                out = jnp.zeros((8, LANES), F32)
                for r in range(blocks):
                    if c == 3:
                        first = 0 if base == 0 else SB
                        row = code_ref[first + r:first + r + 1, :]
                    elif base == 0:
                        row = spos_ref[c:c + 1, r * LANES:(r + 1) * LANES]
                    else:
                        row = pts_ref[c, r:r + 1, :]
                    out = jnp.where(at_block[r], row_gather(row, lane, (8, LANES)), out)
                at = base + c * rows + 8 * m
                rows_ref[at:at + 8] = out
    for i in range(3):
        send_ref[pl.ds(i, DEV, stride=3), :] = rows_ref[i * LANES:(i + 1) * LANES].T


def pack(count, sdest, sslot, spos, mdest, mslot, mface, mnode, coords):
    blocks = SB + MB
    return call(
        pack_body,
        (
            jax.ShapeDtypeStruct((3 * DEV, LANES), F32),
            jax.ShapeDtypeStruct((SB, LANES), I32),
            jax.ShapeDtypeStruct((SB, LANES), I32),
            jax.ShapeDtypeStruct((MB, LANES), I32),
            jax.ShapeDtypeStruct((MB, LANES), I32),
        ),
        [
            pltpu.VMEM((blocks, LANES), F32),
            pltpu.VMEM((blocks, LANES), I32),
            pltpu.VMEM((blocks, LANES), I32),
            pltpu.VMEM((blocks, LANES), F32),
            pltpu.VMEM((LANES, LANES), F32),
            pltpu.VMEM((LANES, LANES), F32),
            pltpu.VMEM((blocks, 16, LANES), F32),
            pltpu.VMEM((3, MB, LANES), F32),
            pltpu.VMEM((3 * LANES, LANES), F32),
        ],
        in_specs=[SM] + [VM] * 8,
        cost=10**9,
    )(count, sdest, sslot, spos, mdest, mslot, mface, mnode, coords)


def order_body(coords_ref, stiff_ref, order_ref, table_ref, inv_ref, src_ref):
    src_ref[0:27] = coords_ref[...]
    src_ref[27:28] = stiff_ref[...]
    src_ref[28:32] = jnp.zeros((4, FT * LANES), F32)
    lanes_bf = iota((FT, LANES), 1).astype(F32).astype(BF16)
    zero = jnp.zeros((FT, LANES), BF16)
    inverse = jnp.zeros((2 * FT, LANES), F32)
    left, right = [], []
    for m in range(FT):
        order = order_ref[m:m + 1, :]
        hi = order >> 7
        lo = order & 127
        lane = jnp.broadcast_to(lo, (8, LANES))
        tile = jnp.broadcast_to(hi, (8, LANES))
        at_tile = [tile == t for t in range(FT)]
        for g in range(4):
            out = jnp.zeros((8, LANES), F32)
            for t in range(FT):
                got = jnp.take_along_axis(
                    src_ref[8 * g:8 * g + 8, t * LANES:(t + 1) * LANES], lane, axis=1
                )
                out = jnp.where(at_tile[t], got, out)
            table_ref[8 * g:8 * g + 8, m * LANES:(m + 1) * LANES] = out
        mine = slot_rows(FT) == wide16(hi, FT)
        left.append(jnp.concatenate([
            jnp.where(mine, jnp.full((FT, LANES), m, BF16), zero), jnp.where(mine, lanes_bf, zero)
        ], 0))
        right.append(one_hot(LANES, lo))
        if m % 4 == 3:
            inverse = inverse + dot_nt(jnp.concatenate(left, 1), jnp.concatenate(right, 1))
            left, right = [], []
    inv_ref[...] = inverse.astype(I32)


def order_faces(coords, stiff, order):
    faces = FT * LANES
    return call(
        order_body,
        (
            jax.ShapeDtypeStruct((32, faces), F32),
            jax.ShapeDtypeStruct((2 * FT, LANES), I32),
        ),
        [pltpu.VMEM((32, faces), F32)],
        cost=10**9,
    )(coords, stiff, order)


def quadratic(low, mid, high):
    return mid, 0.5 * (high - low), 0.5 * (high + low) - mid


def project(point, nodes, stiff):
    coef = []
    for c in range(3):
        by_j = [quadratic(nodes[3 * j][c], nodes[3 * j + 1][c], nodes[3 * j + 2][c]) for j in range(3)]
        coef.append([quadratic(by_j[0][p], by_j[1][p], by_j[2][p]) for p in range(3)])

    def surface(u, v):
        u2 = u + u
        v2 = v + v
        x, tu, tv = [], [], []
        for c in range(3):
            k = coef[c]
            h = [k[0][q] + u * (k[1][q] + u * k[2][q]) for q in range(3)]
            d = [k[1][q] + u2 * k[2][q] for q in range(3)]
            x.append(h[0] + v * (h[1] + v * h[2]))
            tu.append(d[0] + v * (d[1] + v * d[2]))
            tv.append(h[1] + v2 * h[2])
        return x, tu, tv

    def inner(a, b):
        return a[0] * b[0] + a[1] * b[1] + a[2] * b[2]

    u = v = jnp.zeros_like(point[0])
    for step in range(NEWTON):
        if step == 0:
            x = [coef[c][0][0] for c in range(3)]
            tu = [coef[c][1][0] for c in range(3)]
            tv = [coef[c][0][1] for c in range(3)]
        else:
            x, tu, tv = surface(u, v)
        o = [point[c] - x[c] for c in range(3)]
        a_uu, a_uv, a_vv = inner(tu, tu), inner(tu, tv), inner(tv, tv)
        b_u, b_v = inner(tu, o), inner(tv, o)
        scale = 1.0 / (a_uu * a_vv - a_uv * a_uv)
        du = (a_vv * b_u - a_uv * b_v) * scale
        dv = (a_uu * b_v - a_uv * b_u) * scale
        u = jnp.clip(u + du, -CLIP_EDGE, CLIP_EDGE)
        v = jnp.clip(v + dv, -CLIP_EDGE, CLIP_EDGE)
    x, tu, tv = surface(u, v)
    n = [
        tu[1] * tv[2] - tu[2] * tv[1],
        tu[2] * tv[0] - tu[0] * tv[2],
        tu[0] * tv[1] - tu[1] * tv[0],
    ]
    unit = 1.0 / jnp.sqrt(inner(n, n))
    gap = inner([point[c] - x[c] for c in range(3)], n) * unit
    size = 0.5 * stiff * jnp.maximum(-gap, 0.0) * unit
    return u, v, [size * n[c] for c in range(3)]


def force_body(recv_ref, table_ref, back_ref, uv_ref, force_ref, index_ref, rows_ref):
    for i in range(3):
        rows_ref[i * LANES:(i + 1) * LANES] = recv_ref[pl.ds(i, DEV, stride=3), :].T
    shape = (8, LANES)
    upper = iota(shape, 0) < 4
    force_ref[3 * SK + 3 * MK:] = jnp.zeros((LANES - 32, LANES), F32)
    for g in range(12):
        if g < 8:
            at = [c * SK + g * 8 for c in range(4)]
            out = [c * SK + g * 8 for c in range(3)]
        else:
            at = [4 * SK + c * MK + (g - 8) * 8 for c in range(4)]
            out = [3 * SK + c * MK + (g - 8) * 8 for c in range(3)]
        point = [rows_ref[at[c]:at[c] + 8, :] for c in range(3)]
        code = rows_ref[at[3]:at[3] + 8, :].astype(I32)
        index = jnp.maximum(code - 1, 0)
        lane = index & 127
        high = index >= LANES

        def entry(row, half):
            def tile(t):
                return jnp.broadcast_to(table_ref[row:row + 1, t * LANES:(t + 1) * LANES], shape)

            if g < 8:
                return tile(2 * g + half)
            first = 4 * (g - 8)
            return jnp.where(upper, tile(first + half), tile(first + 2 + half))

        def pick(row):
            got = [jnp.take_along_axis(entry(row, half), lane, axis=1) for half in range(2)]
            return jnp.where(high, got[1], got[0])

        nodes = [[pick(3 * a + c) for c in range(3)] for a in range(9)]
        stiff = jnp.where(code > 0, pick(27), 0.0)
        u, v, force = project(point, nodes, stiff)
        uv_ref[g * 8:g * 8 + 8] = u
        uv_ref[96 + g * 8:96 + g * 8 + 8] = v
        index_ref[g * 8:g * 8 + 8] = index
        for c in range(3):
            force_ref[out[c]:out[c] + 8] = force[c]
    for i in range(3):
        back_ref[pl.ds(i, DEV, stride=3), :] = force_ref[i * LANES:(i + 1) * LANES].T


def forces(recv, table):
    return call(
        force_body,
        (
            jax.ShapeDtypeStruct((3 * DEV, LANES), F32),
            jax.ShapeDtypeStruct((192, LANES), F32),
            jax.ShapeDtypeStruct((3 * LANES, LANES), F32),
            jax.ShapeDtypeStruct((96, LANES), I32),
        ),
        [pltpu.VMEM((3 * LANES, LANES), F32)],
        cost=10**9,
    )(recv, table)


def split(x):
    high = x.astype(BF16)
    return high, (x - high.astype(F32)).astype(BF16)


def react_body(uv_ref, force_ref, index_ref, inv_ref, out_ref, part_ref, sum_ref):
    part_ref[27 * 8:] = jnp.zeros((40, LANES), F32)

    def pieces(g, first, count):
        left, right = [], []
        for k in range(first, first + count):
            left.append(jnp.concatenate(split(part_ref[pl.ds(k, 32, stride=8), :]), 0))
            right.append(one_hot(2 * LANES, index_ref[g * 8 + k:g * 8 + k + 1, :]))
        return dot_nt(jnp.concatenate(left, 1), jnp.concatenate(right, 1))

    def reactions(g):
        u = uv_ref[g * 8:g * 8 + 8]
        v = uv_ref[96 + g * 8:96 + g * 8 + 8]
        lu = (u * (u - 1.0) * 0.5, 1.0 - u * u, u * (u + 1.0) * 0.5)
        lv = (v * (v - 1.0) * 0.5, 1.0 - v * v, v * (v + 1.0) * 0.5)
        for c in range(3):
            row = c * SK + g * 8 if g < 8 else 3 * SK + c * MK + (g - 8) * 8
            f = -force_ref[row:row + 8]
            for j in range(3):
                fj = f * lv[j]
                for i in range(3):
                    a = 3 * (i + 3 * j) + c
                    part_ref[a * 8:a * 8 + 8] = lu[i] * fj

    mirrored = []
    for m in range(4):
        reactions(8 + m)
        mirrored += [pieces(8 + m, 0, 4), pieces(8 + m, 4, 4)]
        for b in (2 * m, 2 * m + 1):
            reactions(b)
            both = mirrored[b] + pieces(b, 0, 8)
            sum_ref[:, b * 256:(b + 1) * 256] = both[0:32] + both[32:64]

    for m in range(FT):
        hi = inv_ref[m:m + 1, :]
        lane = jnp.broadcast_to(inv_ref[FT + m:FT + m + 1, :], (8, LANES))
        tile = jnp.broadcast_to(hi, (8, LANES))
        at_tile = [tile == t for t in range(FT)]
        for g in range(4):
            out = jnp.zeros((8, LANES), F32)
            for t in range(FT):
                got = jnp.take_along_axis(
                    sum_ref[8 * g:8 * g + 8, t * LANES:(t + 1) * LANES], lane, axis=1
                )
                out = jnp.where(at_tile[t], got, out)
            out_ref[8 * g:8 * g + 8, m * LANES:(m + 1) * LANES] = out


def react(uv, force, index, inv):
    return call(
        react_body,
        jax.ShapeDtypeStruct((32, FT * LANES), F32),
        [
            pltpu.VMEM((256, LANES), F32),
            pltpu.VMEM((32, FT * LANES), F32),
        ],
        cost=10**9,
    )(uv, force, index, inv)


def finish_body(
    back_ref, speer_ref, sk_ref, mpeer_ref, mk_ref, mface_ref, mnode_ref, part_ref,
    slave_ref, face_ref, rows_ref, own_ref,
):
    for i in range(3):
        rows_ref[i * LANES:(i + 1) * LANES] = back_ref[pl.ds(i, DEV, stride=3), :].T

    def collect(peer, slot, base, slots):
        at_slot = [slot == k for k in range(slots)]
        for c in range(3):
            out = jnp.zeros((8, LANES), F32)
            for k in range(slots):
                row = base + c * slots + k
                out = jnp.where(at_slot[k], row_gather(rows_ref[row:row + 1, :], peer, (8, LANES)), out)
            yield c, out

    for m in range(MB // 8):
        for c, out in collect(mpeer_ref[8 * m:8 * m + 8], mk_ref[8 * m:8 * m + 8], 3 * SK, MK):
            own_ref[c, 8 * m:8 * m + 8] = out

    sub = iota((32, LANES), 0)
    comp = sub % 3
    node = sub // 3
    zero = jnp.zeros((64, LANES), BF16)
    both = jnp.zeros((8 * 64, 2 * LANES), F32)
    left, right = [], []
    for r in range(MB):
        f = jnp.where(comp == 0, own_ref[0, r:r + 1, :], own_ref[1, r:r + 1, :])
        f = jnp.where(comp == 2, own_ref[2, r:r + 1, :], f)
        f = jnp.where(node == mnode_ref[r:r + 1, :], f, 0.0)
        f = jnp.concatenate(split(f), 0)
        face = mface_ref[r:r + 1, :]
        high = wide16(face >> 8, 64)
        left.append(jnp.concatenate(
            [jnp.where(high == jnp.full((64, LANES), h, I16), f, zero) for h in range(8)], 0
        ))
        right.append(one_hot(2 * LANES, face & 255))
        if r % 2 == 1:
            both = both + dot_nt(jnp.concatenate(left, 1), jnp.concatenate(right, 1))
            left, right = [], []
    for h in range(8):
        at = slice(h * 256, (h + 1) * 256)
        share = both[64 * h:64 * h + 32] + both[64 * h + 32:64 * h + 64]
        face_ref[:, at] = (part_ref[:, at] + share)[0:27]

    for m in range(SB // 8):
        for c, out in collect(speer_ref[8 * m:8 * m + 8], sk_ref[8 * m:8 * m + 8], 0, SK):
            for r in range(8):
                at = (8 * m + r) * LANES
                slave_ref[c:c + 1, at:at + LANES] = out[r:r + 1, :]


def finish(back, speer, sk, mpeer, mk, mface, mnode, part):
    return call(
        finish_body,
        (
            jax.ShapeDtypeStruct((3, SB * LANES), F32),
            jax.ShapeDtypeStruct((27, FT * LANES), F32),
        ),
        [
            pltpu.VMEM((3 * LANES, LANES), F32),
            pltpu.VMEM((3, MB, LANES), F32),
        ],
        cost=10**9,
    )(back, speer, sk, mpeer, mk, mface, mnode, part)


def exchange(x):
    x = x.reshape(DEV, 1, 3 * LANES)
    x = lax.all_to_all(x, ("mech", "bin"), split_axis=0, concat_axis=0, tiled=True)
    return x.reshape(3 * DEV, LANES)


def shards(
    face_coords, face_stiff, bin_order, slave_pos, slave_dest, face_slot, block_count,
    mirror_face, mirror_node, mirror_dest, mirror_slot,
):
    mface = mirror_face.reshape(MB, LANES)
    mnode = mirror_node.reshape(MB, LANES)
    send, speer, sk, mpeer, mk = pack(
        block_count,
        slave_dest.reshape(SB, LANES),
        face_slot.reshape(SB, LANES),
        slave_pos,
        mirror_dest.reshape(MB, LANES),
        mirror_slot.reshape(MB, LANES),
        mface,
        mnode,
        face_coords,
    )
    recv = exchange(send)
    table, inv = order_faces(
        face_coords, face_stiff.reshape(1, FT * LANES), bin_order.reshape(FT, LANES)
    )
    back, uv, force, index = forces(recv, table)
    returned = exchange(back)
    part = react(uv, force, index, inv)
    return finish(returned, speer, sk, mpeer, mk, mface, mnode, part)


def solution(mesh):
    axes = ("mech", "bin")
    return jax.shard_map(
        shards,
        mesh=mesh,
        in_specs=(
            P(None, axes), P(axes), P(axes, None), P(None, axes), P(axes, None), P(axes),
            P(axes, None), P(axes), P(axes), P(axes, None), P(axes),
        ),
        out_specs=(P(None, axes), P(None, axes)),
        check_vma=False,
    )
```

```python
import functools

import jax
import jax.numpy as jnp
from jax import lax
from jax.experimental import pallas as pl
from jax.experimental.pallas import tpu as pltpu
from jax.sharding import PartitionSpec as P

NEWTON = 5
CLIP_EDGE = 1.1
VMEM_BYTES = 16 * 2**20
F32 = jnp.float32
BF16 = jnp.bfloat16
I32 = jnp.int32
I16 = jnp.int16
LANES = 128
SB = 32
MB = 16
FT = 16
DEV = 128
NBIN = 8
SK = 64
MK = 32


def iota(shape, dim):
    return lax.broadcasted_iota(I32, shape, dim)


def dot_nt(a, b):
    return lax.dot_general(a, b, (((1,), (1,)), ((), ())), preferred_element_type=F32)


def wide16(row, rows):
    narrow = jnp.broadcast_to(row, (16, LANES)).astype(I16)
    return jnp.concatenate([narrow] * (rows // 16), 0) if rows > 16 else narrow


def slot_rows(rows):
    return iota((rows, LANES), 0).astype(I16)


def pick_bf16(rows16, row):
    hit = rows16 == wide16(row, rows16.shape[0])
    return jnp.where(hit, jnp.ones(rows16.shape, BF16), jnp.zeros(rows16.shape, BF16))


def one_hot(rows, row):
    return pick_bf16(slot_rows(rows), row)


def row_gather(row, lane, shape):
    return jnp.take_along_axis(jnp.broadcast_to(row, shape), lane, axis=1)


def call(body, out_shape, scratch=(), in_specs=None, cost=0, vmem=VMEM_BYTES):
    kwargs = {} if in_specs is None else {"in_specs": in_specs}
    return pl.pallas_call(
        body,
        out_shape=out_shape,
        scratch_shapes=list(scratch),
        compiler_params=pltpu.CompilerParams(vmem_limit_bytes=vmem),
        cost_estimate=pl.CostEstimate(flops=cost, bytes_accessed=cost // 100, transcendentals=0),
        **kwargs,
    )


VM = pl.BlockSpec(memory_space=pltpu.VMEM)
SM = pl.BlockSpec(memory_space=pltpu.SMEM)
HB = pl.BlockSpec(memory_space=pltpu.HBM)


def pack_body(
    count_ref, *refs,
):
    sources, refs = refs[:8], refs[8:]
    send_ref, speer_ref, sk_ref, mpeer_ref, mk_ref = refs[:5]
    buffers, refs = refs[5:13], refs[13:]
    sdest_ref, sslot_ref, mdest_ref, mslot_ref, mface_ref, mnode_ref, coords_ref, spos_ref = buffers
    e_ref, b_ref, val_ref, turn_ref, cols_ref, cnt_ref, rows_ref, sems = refs
    copies = [
        pltpu.make_async_copy(sources[i], buffers[i], sems.at[i]) for i in range(8)
    ]
    for copy in copies:
        copy.start()
    for copy in copies:
        copy.wait()

    def keys(dest, slot):
        owner = (dest & ~(NBIN - 1)) | (slot >> 8)
        return owner, dest & (NBIN - 1), (slot & 255) + 1

    half = LANES // 2
    for first, rows, dest_ref, slot_ref, peer_ref in (
        (0, SB, sdest_ref, sslot_ref, speer_ref),
        (SB, MB, mdest_ref, mslot_ref, mpeer_ref),
    ):
        owner, col, code = keys(dest_ref[...], slot_ref[...])
        e_ref[first:first + rows] = owner
        b_ref[first:first + rows] = col
        val_ref[6, first:first + rows] = code.astype(F32)
        peer_ref[...] = owner
        cell = (owner * NBIN + col).astype(F32)
        turn_ref[first:first + rows] = cell
        turn_ref[half + first:half + first + rows] = pltpu.roll(cell, half, axis=1)
    for first in (SB + MB, half + SB + MB):
        turn_ref[first:first + half - SB - MB] = jnp.zeros((half - SB - MB, LANES), F32)
    cols_ref[...] = turn_ref[...].T

    lane_row = iota((1, LANES), 1)
    lane8 = iota((NBIN, LANES), 1)
    earlier = iota((half, LANES), 0) < (iota((half, LANES), 1) & (half - 1))
    sub8 = iota((NBIN, LANES), 0)
    upper = lane8 >= half
    row16 = iota((16, LANES), 0)
    bin_rows = jnp.where((row16 < 8) | (iota((16, LANES), 1) < half), row16 & 7, -1).astype(I16)

    for r in range(SB + MB):
        bins = pick_bf16(bin_rows, b_ref[r:r + 1, :])
        cnt_ref[r] = dot_nt(bins, one_hot(LANES, e_ref[r:r + 1, :]))

    for m in range(MB // 8):
        face = mface_ref[8 * m:8 * m + 8]
        tile = face >> 7
        lane = face & 127
        node = mnode_ref[8 * m:8 * m + 8]
        at_tile = [tile == t for t in range(FT)]
        for c in range(3):
            point = jnp.zeros((8, LANES), F32)
            for n in range(9):
                part = jnp.zeros((8, LANES), F32)
                for t in range(FT):
                    got = row_gather(
                        coords_ref[3 * n + c:3 * n + c + 1, t * LANES:(t + 1) * LANES], lane, (8, LANES)
                    )
                    part = jnp.where(at_tile[t], got, part)
                point = jnp.where(node == n, part, point)
            high = point.astype(BF16).astype(F32)
            val_ref[c, SB + 8 * m:SB + 8 * m + 8] = high
            val_ref[3 + c, SB + 8 * m:SB + 8 * m + 8] = point - high

    def value(i, r):
        if r >= SB or i == 6:
            return val_ref[i, r:r + 1, :]
        x = spos_ref[i % 3:i % 3 + 1, r * LANES:(r + 1) * LANES]
        high = x.astype(BF16).astype(F32)
        return high if i < 3 else x - high

    def slots(first, last, cap, rows, kout):
        seen = jnp.zeros((NBIN, LANES), F32)
        total = jnp.zeros((7 * rows, LANES), F32)
        zero = jnp.zeros((rows, LANES), BF16)
        for group in range(first, last, 4):
            left, right = [], []
            for r in range(group, group + 4):
                i = r - first
                peers = jnp.broadcast_to(e_ref[r:r + 1, :], (NBIN, LANES))
                column = jnp.where(upper, half + r, r)
                before = jnp.take_along_axis(seen, peers, axis=1) + jnp.where(
                    upper, jnp.take_along_axis(cnt_ref[r, 8:16], peers, axis=1), 0.0
                )
                before = jnp.where(sub8 == b_ref[r:r + 1, :], before, 0.0)
                for m in range(half // 8):
                    col = jnp.take_along_axis(cols_ref[8 * m:8 * m + 8], column, axis=1)
                    same = (turn_ref[r:r + 1, :] == col) & earlier[8 * m:8 * m + 8]
                    before = before + jnp.where(same, 1.0, 0.0)
                rank = jnp.sum(before, 0, keepdims=True)
                k = b_ref[r:r + 1, :] * cap + rank.astype(I32)
                if first == 0:
                    k = jnp.where(lane_row < count_ref[0, i], k, -1)
                kout[i:i + 1, :] = k
                mine = slot_rows(rows) == wide16(k, rows)
                parts = []
                for j in (0, 1, 2, 6, 3, 4, 5):
                    x = jnp.broadcast_to(value(j, r), (16, LANES)).astype(BF16)
                    parts.append(jnp.where(mine, jnp.concatenate([x] * (rows // 16), 0), zero))
                left.append(jnp.concatenate(parts, 0))
                right.append(one_hot(LANES, e_ref[r:r + 1, :]))
                seen = seen + cnt_ref[r, 0:8]
            total = total + dot_nt(jnp.concatenate(left, 1), jnp.concatenate(right, 1))
        return jnp.concatenate([total[0:3 * rows] + total[4 * rows:], total[3 * rows:4 * rows]], 0)

    rows_ref[0:4 * SK] = slots(0, SB, 8, SK, sk_ref)
    rows_ref[4 * SK:] = slots(SB, SB + MB, 4, MK, mk_ref)
    for i in range(3):
        send_ref[pl.ds(i, DEV, stride=3), :] = rows_ref[i * LANES:(i + 1) * LANES].T


def pack(count, sdest, sslot, spos, mdest, mslot, mface, mnode, coords):
    blocks = SB + MB
    arrays = (sdest, sslot, mdest, mslot, mface, mnode, coords, spos)
    return call(
        pack_body,
        (
            jax.ShapeDtypeStruct((3 * DEV, LANES), F32),
            jax.ShapeDtypeStruct((SB, LANES), I32),
            jax.ShapeDtypeStruct((SB, LANES), I32),
            jax.ShapeDtypeStruct((MB, LANES), I32),
            jax.ShapeDtypeStruct((MB, LANES), I32),
        ),
        [pltpu.VMEM(x.shape, x.dtype) for x in arrays] + [
            pltpu.VMEM((blocks, LANES), I32),
            pltpu.VMEM((blocks, LANES), I32),
            pltpu.VMEM((7, blocks, LANES), F32),
            pltpu.VMEM((LANES, LANES), F32),
            pltpu.VMEM((LANES, LANES), F32),
            pltpu.VMEM((blocks, 16, LANES), F32),
            pltpu.VMEM((3 * LANES, LANES), F32),
            pltpu.SemaphoreType.DMA((8,)),
        ],
        in_specs=[SM] + [HB] * 8,
        cost=10**9,
        vmem=60 * 1024 * 1024,
    )(count, *arrays)


def quadratic(low, mid, high):
    return mid, 0.5 * (high - low), 0.5 * (high + low) - mid


def order_body(coords_ref, stiff_ref, order_ref, table_ref, inv_ref, src_ref):
    for c in range(3):
        node = [coords_ref[3 * a + c:3 * a + c + 1, :] for a in range(9)]
        by_j = [quadratic(*node[3 * j:3 * j + 3]) for j in range(3)]
        for p in range(3):
            for q, value in enumerate(quadratic(by_j[0][p], by_j[1][p], by_j[2][p])):
                row = 9 * c + 3 * p + q
                src_ref[row:row + 1] = value
    src_ref[27:28] = stiff_ref[...]
    src_ref[28:32] = jnp.zeros((4, FT * LANES), F32)
    lanes_bf = iota((FT, LANES), 1).astype(F32).astype(BF16)
    zero = jnp.zeros((FT, LANES), BF16)
    inverse = jnp.zeros((2 * FT, LANES), F32)
    left, right = [], []
    for m in range(FT):
        order = order_ref[m:m + 1, :]
        hi = order >> 7
        lo = order & 127
        lane = jnp.broadcast_to(lo, (8, LANES))
        tile = jnp.broadcast_to(hi, (8, LANES))
        at_tile = [tile == t for t in range(FT)]
        for g in range(4):
            out = jnp.zeros((8, LANES), F32)
            for t in range(FT):
                got = jnp.take_along_axis(
                    src_ref[8 * g:8 * g + 8, t * LANES:(t + 1) * LANES], lane, axis=1
                )
                out = jnp.where(at_tile[t], got, out)
            table_ref[8 * g:8 * g + 8, m * LANES:(m + 1) * LANES] = out
        mine = slot_rows(FT) == wide16(hi, FT)
        left.append(jnp.concatenate([
            jnp.where(mine, jnp.full((FT, LANES), m, BF16), zero), jnp.where(mine, lanes_bf, zero)
        ], 0))
        right.append(one_hot(LANES, lo))
        if m % 4 == 3:
            inverse = inverse + dot_nt(jnp.concatenate(left, 1), jnp.concatenate(right, 1))
            left, right = [], []
    inv_ref[...] = inverse.astype(I32)


def order_faces(coords, stiff, order):
    faces = FT * LANES
    return call(
        order_body,
        (
            jax.ShapeDtypeStruct((32, faces), F32),
            jax.ShapeDtypeStruct((2 * FT, LANES), I32),
        ),
        [pltpu.VMEM((32, faces), F32)],
        cost=10**9,
    )(coords, stiff, order)


def project(point, coef, stiff):
    def surface(u, v):
        u2 = u + u
        v2 = v + v
        x, tu, tv = [], [], []
        for c in range(3):
            k = coef[c]
            h = [k[0][q] + u * (k[1][q] + u * k[2][q]) for q in range(3)]
            d = [k[1][q] + u2 * k[2][q] for q in range(3)]
            x.append(h[0] + v * (h[1] + v * h[2]))
            tu.append(d[0] + v * (d[1] + v * d[2]))
            tv.append(h[1] + v2 * h[2])
        return x, tu, tv

    def inner(a, b):
        return a[0] * b[0] + a[1] * b[1] + a[2] * b[2]

    u = v = jnp.zeros_like(point[0])
    for step in range(NEWTON):
        if step == 0:
            x = [coef[c][0][0] for c in range(3)]
            tu = [coef[c][1][0] for c in range(3)]
            tv = [coef[c][0][1] for c in range(3)]
        else:
            x, tu, tv = surface(u, v)
        o = [point[c] - x[c] for c in range(3)]
        a_uu, a_uv, a_vv = inner(tu, tu), inner(tu, tv), inner(tv, tv)
        b_u, b_v = inner(tu, o), inner(tv, o)
        scale = 1.0 / (a_uu * a_vv - a_uv * a_uv)
        du = (a_vv * b_u - a_uv * b_v) * scale
        dv = (a_uu * b_v - a_uv * b_u) * scale
        u = jnp.clip(u + du, -CLIP_EDGE, CLIP_EDGE)
        v = jnp.clip(v + dv, -CLIP_EDGE, CLIP_EDGE)
    x, tu, tv = surface(u, v)
    n = [
        tu[1] * tv[2] - tu[2] * tv[1],
        tu[2] * tv[0] - tu[0] * tv[2],
        tu[0] * tv[1] - tu[1] * tv[0],
    ]
    unit = 1.0 / jnp.sqrt(inner(n, n))
    gap = inner([point[c] - x[c] for c in range(3)], n) * unit
    size = 0.5 * stiff * jnp.maximum(-gap, 0.0) * unit
    return u, v, [size * n[c] for c in range(3)]


def force_body(recv_ref, table_ref, back_ref, uv_ref, force_ref, index_ref, rows_ref):
    for i in range(3):
        rows_ref[i * LANES:(i + 1) * LANES] = recv_ref[pl.ds(i, DEV, stride=3), :].T
    shape = (8, LANES)
    upper = iota(shape, 0) < 4
    force_ref[3 * SK + 3 * MK:] = jnp.zeros((LANES - 32, LANES), F32)
    for g in range(12):
        if g < 8:
            at = [c * SK + g * 8 for c in range(4)]
            out = [c * SK + g * 8 for c in range(3)]
        else:
            at = [4 * SK + c * MK + (g - 8) * 8 for c in range(4)]
            out = [3 * SK + c * MK + (g - 8) * 8 for c in range(3)]
        point = [rows_ref[at[c]:at[c] + 8, :] for c in range(3)]
        code = rows_ref[at[3]:at[3] + 8, :].astype(I32)
        index = jnp.maximum(code - 1, 0)
        lane = index & 127
        high = index >= LANES

        def entry(row, half):
            def tile(t):
                return jnp.broadcast_to(table_ref[row:row + 1, t * LANES:(t + 1) * LANES], shape)

            if g < 8:
                return tile(2 * g + half)
            first = 4 * (g - 8)
            return jnp.where(upper, tile(first + half), tile(first + 2 + half))

        def pick(row):
            got = [jnp.take_along_axis(entry(row, half), lane, axis=1) for half in range(2)]
            return jnp.where(high, got[1], got[0])

        coef = [[[pick(9 * c + 3 * p + q) for q in range(3)] for p in range(3)] for c in range(3)]
        stiff = jnp.where(code > 0, pick(27), 0.0)
        u, v, force = project(point, coef, stiff)
        uv_ref[g * 8:g * 8 + 8] = u
        uv_ref[96 + g * 8:96 + g * 8 + 8] = v
        index_ref[g * 8:g * 8 + 8] = index
        for c in range(3):
            force_ref[out[c]:out[c] + 8] = force[c]
    for i in range(3):
        back_ref[pl.ds(i, DEV, stride=3), :] = force_ref[i * LANES:(i + 1) * LANES].T


def forces(recv, table):
    return call(
        force_body,
        (
            jax.ShapeDtypeStruct((3 * DEV, LANES), F32),
            jax.ShapeDtypeStruct((192, LANES), F32),
            jax.ShapeDtypeStruct((3 * LANES, LANES), F32),
            jax.ShapeDtypeStruct((96, LANES), I32),
        ),
        [pltpu.VMEM((3 * LANES, LANES), F32)],
        cost=10**9,
    )(recv, table)


def split(x):
    high = x.astype(BF16)
    return high, (x - high.astype(F32)).astype(BF16)


def react_body(uv_ref, force_ref, index_ref, inv_ref, out_ref, part_ref, sum_ref):
    part_ref[27 * 8:] = jnp.zeros((40, LANES), F32)

    def pieces(g, first, count):
        left, right = [], []
        for k in range(first, first + count):
            left.append(jnp.concatenate(split(part_ref[pl.ds(k, 32, stride=8), :]), 0))
            right.append(one_hot(2 * LANES, index_ref[g * 8 + k:g * 8 + k + 1, :]))
        return dot_nt(jnp.concatenate(left, 1), jnp.concatenate(right, 1))

    def reactions(g):
        u = uv_ref[g * 8:g * 8 + 8]
        v = uv_ref[96 + g * 8:96 + g * 8 + 8]
        lu = (u * (u - 1.0) * 0.5, 1.0 - u * u, u * (u + 1.0) * 0.5)
        lv = (v * (v - 1.0) * 0.5, 1.0 - v * v, v * (v + 1.0) * 0.5)
        for c in range(3):
            row = c * SK + g * 8 if g < 8 else 3 * SK + c * MK + (g - 8) * 8
            f = -force_ref[row:row + 8]
            for j in range(3):
                fj = f * lv[j]
                for i in range(3):
                    a = 3 * (i + 3 * j) + c
                    part_ref[a * 8:a * 8 + 8] = lu[i] * fj

    mirrored = []
    for m in range(4):
        reactions(8 + m)
        mirrored += [pieces(8 + m, 0, 4), pieces(8 + m, 4, 4)]
        for b in (2 * m, 2 * m + 1):
            reactions(b)
            both = mirrored[b] + pieces(b, 0, 8)
            sum_ref[:, b * 256:(b + 1) * 256] = both[0:32] + both[32:64]

    for m in range(FT):
        hi = inv_ref[m:m + 1, :]
        lane = jnp.broadcast_to(inv_ref[FT + m:FT + m + 1, :], (8, LANES))
        tile = jnp.broadcast_to(hi, (8, LANES))
        at_tile = [tile == t for t in range(FT)]
        for g in range(4):
            out = jnp.zeros((8, LANES), F32)
            for t in range(FT):
                got = jnp.take_along_axis(
                    sum_ref[8 * g:8 * g + 8, t * LANES:(t + 1) * LANES], lane, axis=1
                )
                out = jnp.where(at_tile[t], got, out)
            out_ref[8 * g:8 * g + 8, m * LANES:(m + 1) * LANES] = out


def react(uv, force, index, inv):
    return call(
        react_body,
        jax.ShapeDtypeStruct((32, FT * LANES), F32),
        [
            pltpu.VMEM((256, LANES), F32),
            pltpu.VMEM((32, FT * LANES), F32),
        ],
        cost=10**9,
    )(uv, force, index, inv)


def finish_body(
    back_ref, speer_ref, sk_ref, mpeer_ref, mk_ref, mface_ref, mnode_ref, part_ref,
    slave_ref, face_ref, rows_ref, own_ref,
):
    for i in range(3):
        rows_ref[i * LANES:(i + 1) * LANES] = back_ref[pl.ds(i, DEV, stride=3), :].T

    def collect(peer, slot, base, slots):
        at_slot = [slot == k for k in range(slots)]
        for c in range(3):
            out = jnp.zeros((8, LANES), F32)
            for k in range(slots):
                row = base + c * slots + k
                out = jnp.where(at_slot[k], row_gather(rows_ref[row:row + 1, :], peer, (8, LANES)), out)
            yield c, out

    for m in range(MB // 8):
        for c, out in collect(mpeer_ref[8 * m:8 * m + 8], mk_ref[8 * m:8 * m + 8], 3 * SK, MK):
            own_ref[c, 8 * m:8 * m + 8] = out

    sub = iota((32, LANES), 0)
    comp = sub % 3
    node = sub // 3
    zero = jnp.zeros((64, LANES), BF16)
    both = jnp.zeros((8 * 64, 2 * LANES), F32)
    left, right = [], []
    for r in range(MB):
        f = jnp.where(comp == 0, own_ref[0, r:r + 1, :], own_ref[1, r:r + 1, :])
        f = jnp.where(comp == 2, own_ref[2, r:r + 1, :], f)
        f = jnp.where(node == mnode_ref[r:r + 1, :], f, 0.0)
        f = jnp.concatenate(split(f), 0)
        face = mface_ref[r:r + 1, :]
        high = wide16(face >> 8, 64)
        left.append(jnp.concatenate(
            [jnp.where(high == jnp.full((64, LANES), h, I16), f, zero) for h in range(8)], 0
        ))
        right.append(one_hot(2 * LANES, face & 255))
        if r % 2 == 1:
            both = both + dot_nt(jnp.concatenate(left, 1), jnp.concatenate(right, 1))
            left, right = [], []
    for h in range(8):
        at = slice(h * 256, (h + 1) * 256)
        share = both[64 * h:64 * h + 32] + both[64 * h + 32:64 * h + 64]
        face_ref[:, at] = (part_ref[:, at] + share)[0:27]

    for m in range(SB // 8):
        for c, out in collect(speer_ref[8 * m:8 * m + 8], sk_ref[8 * m:8 * m + 8], 0, SK):
            for r in range(8):
                at = (8 * m + r) * LANES
                slave_ref[c:c + 1, at:at + LANES] = out[r:r + 1, :]


def finish(back, speer, sk, mpeer, mk, mface, mnode, part):
    return call(
        finish_body,
        (
            jax.ShapeDtypeStruct((3, SB * LANES), F32),
            jax.ShapeDtypeStruct((27, FT * LANES), F32),
        ),
        [
            pltpu.VMEM((3 * LANES, LANES), F32),
            pltpu.VMEM((3, MB, LANES), F32),
        ],
        cost=10**9,
    )(back, speer, sk, mpeer, mk, mface, mnode, part)


def exchange(x):
    x = x.reshape(DEV, 1, 3 * LANES)
    x = lax.all_to_all(x, ("mech", "bin"), split_axis=0, concat_axis=0, tiled=True)
    return x.reshape(3 * DEV, LANES)


def shards(
    face_coords, face_stiff, bin_order, slave_pos, slave_dest, face_slot, block_count,
    mirror_face, mirror_node, mirror_dest, mirror_slot,
):
    mface = mirror_face.reshape(MB, LANES)
    mnode = mirror_node.reshape(MB, LANES)
    send, speer, sk, mpeer, mk = pack(
        block_count,
        slave_dest.reshape(SB, LANES),
        face_slot.reshape(SB, LANES),
        slave_pos,
        mirror_dest.reshape(MB, LANES),
        mirror_slot.reshape(MB, LANES),
        mface,
        mnode,
        face_coords,
    )
    recv = exchange(send)
    table, inv = order_faces(
        face_coords, face_stiff.reshape(1, FT * LANES), bin_order.reshape(FT, LANES)
    )
    back, uv, force, index = forces(recv, table)
    returned = exchange(back)
    part = react(uv, force, index, inv)
    return finish(returned, speer, sk, mpeer, mk, mface, mnode, part)


def solution(mesh):
    axes = ("mech", "bin")
    return jax.shard_map(
        shards,
        mesh=mesh,
        in_specs=(
            P(None, axes), P(axes), P(axes, None), P(None, axes), P(axes, None), P(axes),
            P(axes, None), P(axes), P(axes), P(axes, None), P(axes),
        ),
        out_specs=(P(None, axes), P(None, axes)),
        check_vma=False,
    )
```

```python
import functools

import jax
import jax.numpy as jnp
from jax import lax
from jax.experimental import pallas as pl
from jax.experimental.pallas import tpu as pltpu
from jax.sharding import PartitionSpec as P

NEWTON = 5
CLIP_EDGE = 1.1
VMEM_BYTES = 16 * 2**20
F32 = jnp.float32
BF16 = jnp.bfloat16
I32 = jnp.int32
I16 = jnp.int16
LANES = 128
SB = 32
MB = 16
FT = 16
DEV = 128
NBIN = 8
SK = 64
MK = 32


def iota(shape, dim):
    return lax.broadcasted_iota(I32, shape, dim)


def dot_nt(a, b):
    return lax.dot_general(a, b, (((1,), (1,)), ((), ())), preferred_element_type=F32)


def wide16(row, rows):
    narrow = jnp.broadcast_to(row, (16, LANES)).astype(I16)
    return jnp.concatenate([narrow] * (rows // 16), 0) if rows > 16 else narrow


def slot_rows(rows):
    return iota((rows, LANES), 0).astype(I16)


def pick_bf16(rows16, row):
    hit = rows16 == wide16(row, rows16.shape[0])
    return jnp.where(hit, jnp.ones(rows16.shape, BF16), jnp.zeros(rows16.shape, BF16))


def one_hot(rows, row):
    return pick_bf16(slot_rows(rows), row)


def row_gather(row, lane, shape):
    return jnp.take_along_axis(jnp.broadcast_to(row, shape), lane, axis=1)


def call(body, out_shape, scratch=(), in_specs=None, cost=0, vmem=VMEM_BYTES):
    kwargs = {} if in_specs is None else {"in_specs": in_specs}
    return pl.pallas_call(
        body,
        out_shape=out_shape,
        scratch_shapes=list(scratch),
        compiler_params=pltpu.CompilerParams(vmem_limit_bytes=vmem),
        cost_estimate=pl.CostEstimate(flops=cost, bytes_accessed=cost // 100, transcendentals=0),
        **kwargs,
    )


VM = pl.BlockSpec(memory_space=pltpu.VMEM)
HB = pl.BlockSpec(memory_space=pltpu.HBM)


def pack_body(*refs):
    sources, send_ref, keys_ref, buffers, refs = refs[:9], refs[9], refs[10], refs[11:20], refs[20:]
    coords_ref, spos_ref, sdest_ref, sslot_ref, mdest_ref, mslot_ref, mface_ref, mnode_ref, count_ref = buffers
    e_ref, b_ref, val_ref, turn_ref, cols_ref, cnt_ref, rows_ref, sems = refs
    copies = [
        pltpu.make_async_copy(sources[i], buffers[i], sems.at[i]) for i in range(9)
    ]
    for copy in copies:
        copy.start()
    for copy in copies:
        copy.wait()

    def keys(dest, slot):
        owner = (dest & ~(NBIN - 1)) | (slot >> 8)
        return owner, dest & (NBIN - 1), (slot & 255) + 1

    half = LANES // 2
    for first, rows, dest_ref, slot_ref in ((0, SB, sdest_ref, sslot_ref), (SB, MB, mdest_ref, mslot_ref)):
        owner, col, code = keys(dest_ref[...], slot_ref[...])
        e_ref[first:first + rows] = owner
        b_ref[first:first + rows] = col
        val_ref[6, first:first + rows] = code.astype(F32)
        keys_ref[first:first + rows] = owner
        cell = (owner * NBIN + col).astype(F32)
        turn_ref[first:first + rows] = cell
        turn_ref[half + first:half + first + rows] = pltpu.roll(cell, half, axis=1)
    for first in (SB + MB, half + SB + MB):
        turn_ref[first:first + half - SB - MB] = jnp.zeros((half - SB - MB, LANES), F32)
    cols_ref[...] = turn_ref[...].T

    lane_row = iota((1, LANES), 1)
    lane8 = iota((NBIN, LANES), 1)
    earlier = iota((half, LANES), 0) < (iota((half, LANES), 1) & (half - 1))
    sub8 = iota((NBIN, LANES), 0)
    upper = lane8 >= half
    row16 = iota((16, LANES), 0)
    bin_rows = jnp.where((row16 < 8) | (iota((16, LANES), 1) < half), row16 & 7, -1).astype(I16)

    for r in range(SB + MB):
        bins = pick_bf16(bin_rows, b_ref[r:r + 1, :])
        cnt_ref[r] = dot_nt(bins, one_hot(LANES, e_ref[r:r + 1, :]))

    for m in range(MB // 8):
        face = mface_ref[8 * m:8 * m + 8]
        tile = face >> 7
        lane = face & 127
        node = mnode_ref[8 * m:8 * m + 8]
        at_tile = [tile == t for t in range(FT)]
        for c in range(3):
            point = jnp.zeros((8, LANES), F32)
            for n in range(9):
                part = jnp.zeros((8, LANES), F32)
                for t in range(FT):
                    got = row_gather(
                        coords_ref[3 * n + c:3 * n + c + 1, t * LANES:(t + 1) * LANES], lane, (8, LANES)
                    )
                    part = jnp.where(at_tile[t], got, part)
                point = jnp.where(node == n, part, point)
            high = point.astype(BF16).astype(F32)
            val_ref[c, SB + 8 * m:SB + 8 * m + 8] = high
            val_ref[3 + c, SB + 8 * m:SB + 8 * m + 8] = point - high

    def value(i, r):
        if r >= SB or i == 6:
            return val_ref[i, r:r + 1, :]
        x = spos_ref[i % 3:i % 3 + 1, r * LANES:(r + 1) * LANES]
        high = x.astype(BF16).astype(F32)
        return high if i < 3 else x - high

    def slots(first, last, cap, rows):
        seen = jnp.zeros((NBIN, LANES), F32)
        total = jnp.zeros((7 * rows, LANES), F32)
        zero = jnp.zeros((rows, LANES), BF16)
        for group in range(first, last, 4):
            left, right = [], []
            for r in range(group, group + 4):
                i = r - first
                peers = jnp.broadcast_to(e_ref[r:r + 1, :], (NBIN, LANES))
                column = jnp.where(upper, half + r, r)
                before = jnp.take_along_axis(seen, peers, axis=1) + jnp.where(
                    upper, jnp.take_along_axis(cnt_ref[r, 8:16], peers, axis=1), 0.0
                )
                before = jnp.where(sub8 == b_ref[r:r + 1, :], before, 0.0)
                for m in range(half // 8):
                    col = jnp.take_along_axis(cols_ref[8 * m:8 * m + 8], column, axis=1)
                    same = (turn_ref[r:r + 1, :] == col) & earlier[8 * m:8 * m + 8]
                    before = before + jnp.where(same, 1.0, 0.0)
                rank = jnp.sum(before, 0, keepdims=True)
                k = b_ref[r:r + 1, :] * cap + rank.astype(I32)
                if first == 0:
                    k = jnp.where(lane_row < count_ref[0, i], k, -1)
                keys_ref[SB + MB + r:SB + MB + r + 1, :] = k
                mine = slot_rows(rows) == wide16(k, rows)
                parts = []
                for j in (0, 1, 2, 6, 3, 4, 5):
                    x = jnp.broadcast_to(value(j, r), (16, LANES)).astype(BF16)
                    parts.append(jnp.where(mine, jnp.concatenate([x] * (rows // 16), 0), zero))
                left.append(jnp.concatenate(parts, 0))
                right.append(one_hot(LANES, e_ref[r:r + 1, :]))
                seen = seen + cnt_ref[r, 0:8]
            total = total + dot_nt(jnp.concatenate(left, 1), jnp.concatenate(right, 1))
        return jnp.concatenate([total[0:3 * rows] + total[4 * rows:], total[3 * rows:4 * rows]], 0)

    rows_ref[0:4 * SK] = slots(0, SB, 8, SK)
    rows_ref[4 * SK:] = slots(SB, SB + MB, 4, MK)
    for i in range(3):
        send_ref[pl.ds(i, DEV, stride=3), :] = rows_ref[i * LANES:(i + 1) * LANES].T


def pack(count, sdest, sslot, spos, mdest, mslot, mface, mnode, coords):
    blocks = SB + MB
    arrays = (coords, spos, sdest, sslot, mdest, mslot, mface, mnode)
    return call(
        pack_body,
        (
            jax.ShapeDtypeStruct((3 * DEV, LANES), F32),
            jax.ShapeDtypeStruct((2 * blocks, LANES), I32),
        ),
        [pltpu.VMEM(x.shape, x.dtype) for x in arrays] + [
            pltpu.SMEM(count.shape, I32),
            pltpu.VMEM((blocks, LANES), I32),
            pltpu.VMEM((blocks, LANES), I32),
            pltpu.VMEM((7, blocks, LANES), F32),
            pltpu.VMEM((LANES, LANES), F32),
            pltpu.VMEM((LANES, LANES), F32),
            pltpu.VMEM((blocks, 16, LANES), F32),
            pltpu.VMEM((3 * LANES, LANES), F32),
            pltpu.SemaphoreType.DMA((9,)),
        ],
        in_specs=[HB] * 9,
        cost=10**9,
        vmem=60 * 1024 * 1024,
    )(*arrays, count)


def quadratic(low, mid, high):
    return mid, 0.5 * (high - low), 0.5 * (high + low) - mid


def order_body(coords_ref, stiff_ref, order_ref, table_ref, inv_ref, src_ref):
    for c in range(3):
        node = [coords_ref[3 * a + c:3 * a + c + 1, :] for a in range(9)]
        by_j = [quadratic(*node[3 * j:3 * j + 3]) for j in range(3)]
        for p in range(3):
            for q, value in enumerate(quadratic(by_j[0][p], by_j[1][p], by_j[2][p])):
                row = 9 * c + 3 * p + q
                src_ref[row:row + 1] = value
    src_ref[27:28] = stiff_ref[...]
    src_ref[28:32] = jnp.zeros((4, FT * LANES), F32)
    lanes_bf = iota((FT, LANES), 1).astype(F32).astype(BF16)
    zero = jnp.zeros((FT, LANES), BF16)
    inverse = jnp.zeros((2 * FT, LANES), F32)
    left, right = [], []
    for m in range(FT):
        order = order_ref[m:m + 1, :]
        hi = order >> 7
        lo = order & 127
        lane = jnp.broadcast_to(lo, (8, LANES))
        tile = jnp.broadcast_to(hi, (8, LANES))
        at_tile = [tile == t for t in range(FT)]
        for g in range(4):
            out = jnp.zeros((8, LANES), F32)
            for t in range(FT):
                got = jnp.take_along_axis(
                    src_ref[8 * g:8 * g + 8, t * LANES:(t + 1) * LANES], lane, axis=1
                )
                out = jnp.where(at_tile[t], got, out)
            table_ref[8 * g:8 * g + 8, m * LANES:(m + 1) * LANES] = out
        mine = slot_rows(FT) == wide16(hi, FT)
        left.append(jnp.concatenate([
            jnp.where(mine, jnp.full((FT, LANES), m, BF16), zero), jnp.where(mine, lanes_bf, zero)
        ], 0))
        right.append(one_hot(LANES, lo))
        if m % 4 == 3:
            inverse = inverse + dot_nt(jnp.concatenate(left, 1), jnp.concatenate(right, 1))
            left, right = [], []
    inv_ref[...] = inverse.astype(I32)


def order_faces(coords, stiff, order):
    faces = FT * LANES
    return call(
        order_body,
        (
            jax.ShapeDtypeStruct((32, faces), F32),
            jax.ShapeDtypeStruct((2 * FT, LANES), I32),
        ),
        [pltpu.VMEM((32, faces), F32)],
        cost=10**9,
    )(coords, stiff, order)


def project(point, coef, stiff):
    def surface(u, v):
        u2 = u + u
        v2 = v + v
        x, tu, tv = [], [], []
        for c in range(3):
            k = coef[c]
            h = [k[0][q] + u * (k[1][q] + u * k[2][q]) for q in range(3)]
            d = [k[1][q] + u2 * k[2][q] for q in range(3)]
            x.append(h[0] + v * (h[1] + v * h[2]))
            tu.append(d[0] + v * (d[1] + v * d[2]))
            tv.append(h[1] + v2 * h[2])
        return x, tu, tv

    def inner(a, b):
        return a[0] * b[0] + a[1] * b[1] + a[2] * b[2]

    u = v = jnp.zeros_like(point[0])
    for step in range(NEWTON):
        if step == 0:
            x = [coef[c][0][0] for c in range(3)]
            tu = [coef[c][1][0] for c in range(3)]
            tv = [coef[c][0][1] for c in range(3)]
        else:
            x, tu, tv = surface(u, v)
        o = [point[c] - x[c] for c in range(3)]
        a_uu, a_uv, a_vv = inner(tu, tu), inner(tu, tv), inner(tv, tv)
        b_u, b_v = inner(tu, o), inner(tv, o)
        scale = 1.0 / (a_uu * a_vv - a_uv * a_uv)
        du = (a_vv * b_u - a_uv * b_v) * scale
        dv = (a_uu * b_v - a_uv * b_u) * scale
        u = jnp.clip(u + du, -CLIP_EDGE, CLIP_EDGE)
        v = jnp.clip(v + dv, -CLIP_EDGE, CLIP_EDGE)
    x, tu, tv = surface(u, v)
    n = [
        tu[1] * tv[2] - tu[2] * tv[1],
        tu[2] * tv[0] - tu[0] * tv[2],
        tu[0] * tv[1] - tu[1] * tv[0],
    ]
    unit = 1.0 / jnp.sqrt(inner(n, n))
    gap = inner([point[c] - x[c] for c in range(3)], n) * unit
    size = 0.5 * stiff * jnp.maximum(-gap, 0.0) * unit
    return u, v, [size * n[c] for c in range(3)]


def force_body(recv_ref, table_ref, back_ref, uv_ref, force_ref, index_ref, rows_ref):
    for i in range(3):
        rows_ref[i * LANES:(i + 1) * LANES] = recv_ref[pl.ds(i, DEV, stride=3), :].T
    shape = (8, LANES)
    upper = iota(shape, 0) < 4
    force_ref[3 * SK + 3 * MK:] = jnp.zeros((LANES - 32, LANES), F32)
    for g in range(12):
        if g < 8:
            at = [c * SK + g * 8 for c in range(4)]
            out = [c * SK + g * 8 for c in range(3)]
        else:
            at = [4 * SK + c * MK + (g - 8) * 8 for c in range(4)]
            out = [3 * SK + c * MK + (g - 8) * 8 for c in range(3)]
        point = [rows_ref[at[c]:at[c] + 8, :] for c in range(3)]
        code = rows_ref[at[3]:at[3] + 8, :].astype(I32)
        index = jnp.maximum(code - 1, 0)
        lane = index & 127
        high = index >= LANES

        def entry(row, half):
            def tile(t):
                return jnp.broadcast_to(table_ref[row:row + 1, t * LANES:(t + 1) * LANES], shape)

            if g < 8:
                return tile(2 * g + half)
            first = 4 * (g - 8)
            return jnp.where(upper, tile(first + half), tile(first + 2 + half))

        def pick(row):
            got = [jnp.take_along_axis(entry(row, half), lane, axis=1) for half in range(2)]
            return jnp.where(high, got[1], got[0])

        coef = [[[pick(9 * c + 3 * p + q) for q in range(3)] for p in range(3)] for c in range(3)]
        stiff = jnp.where(code > 0, pick(27), 0.0)
        u, v, force = project(point, coef, stiff)
        uv_ref[g * 8:g * 8 + 8] = u
        uv_ref[96 + g * 8:96 + g * 8 + 8] = v
        index_ref[g * 8:g * 8 + 8] = index
        for c in range(3):
            force_ref[out[c]:out[c] + 8] = force[c]
    for i in range(3):
        back_ref[pl.ds(i, DEV, stride=3), :] = force_ref[i * LANES:(i + 1) * LANES].T


def forces(recv, table):
    return call(
        force_body,
        (
            jax.ShapeDtypeStruct((3 * DEV, LANES), F32),
            jax.ShapeDtypeStruct((192, LANES), F32),
            jax.ShapeDtypeStruct((3 * LANES, LANES), F32),
            jax.ShapeDtypeStruct((96, LANES), I32),
        ),
        [pltpu.VMEM((3 * LANES, LANES), F32)],
        cost=10**9,
    )(recv, table)


def split(x):
    high = x.astype(BF16)
    return high, (x - high.astype(F32)).astype(BF16)


def react_body(uv_ref, force_ref, index_ref, inv_ref, out_ref, part_ref, sum_ref):
    part_ref[27 * 8:] = jnp.zeros((40, LANES), F32)

    def pieces(g, first, count):
        left, right = [], []
        for k in range(first, first + count):
            left.append(jnp.concatenate(split(part_ref[pl.ds(k, 32, stride=8), :]), 0))
            right.append(one_hot(2 * LANES, index_ref[g * 8 + k:g * 8 + k + 1, :]))
        return dot_nt(jnp.concatenate(left, 1), jnp.concatenate(right, 1))

    def reactions(g):
        u = uv_ref[g * 8:g * 8 + 8]
        v = uv_ref[96 + g * 8:96 + g * 8 + 8]
        lu = (u * (u - 1.0) * 0.5, 1.0 - u * u, u * (u + 1.0) * 0.5)
        lv = (v * (v - 1.0) * 0.5, 1.0 - v * v, v * (v + 1.0) * 0.5)
        for c in range(3):
            row = c * SK + g * 8 if g < 8 else 3 * SK + c * MK + (g - 8) * 8
            f = -force_ref[row:row + 8]
            for j in range(3):
                fj = f * lv[j]
                for i in range(3):
                    a = 3 * (i + 3 * j) + c
                    part_ref[a * 8:a * 8 + 8] = lu[i] * fj

    mirrored = []
    for m in range(4):
        reactions(8 + m)
        mirrored += [pieces(8 + m, 0, 4), pieces(8 + m, 4, 4)]
        for b in (2 * m, 2 * m + 1):
            reactions(b)
            both = mirrored[b] + pieces(b, 0, 8)
            sum_ref[:, b * 256:(b + 1) * 256] = both[0:32] + both[32:64]

    for m in range(FT):
        hi = inv_ref[m:m + 1, :]
        lane = jnp.broadcast_to(inv_ref[FT + m:FT + m + 1, :], (8, LANES))
        tile = jnp.broadcast_to(hi, (8, LANES))
        at_tile = [tile == t for t in range(FT)]
        for g in range(4):
            out = jnp.zeros((8, LANES), F32)
            for t in range(FT):
                got = jnp.take_along_axis(
                    sum_ref[8 * g:8 * g + 8, t * LANES:(t + 1) * LANES], lane, axis=1
                )
                out = jnp.where(at_tile[t], got, out)
            out_ref[8 * g:8 * g + 8, m * LANES:(m + 1) * LANES] = out


def react(uv, force, index, inv):
    return call(
        react_body,
        jax.ShapeDtypeStruct((32, FT * LANES), F32),
        [
            pltpu.VMEM((256, LANES), F32),
            pltpu.VMEM((32, FT * LANES), F32),
        ],
        cost=10**9,
    )(uv, force, index, inv)


def finish_body(
    back_ref, keys_ref, mface_ref, mnode_ref, part_ref,
    slave_ref, face_ref, rows_ref, own_ref,
):
    for i in range(3):
        rows_ref[i * LANES:(i + 1) * LANES] = back_ref[pl.ds(i, DEV, stride=3), :].T

    def collect(block, base, slots):
        peer = keys_ref[block:block + 8]
        slot = keys_ref[SB + MB + block:SB + MB + block + 8]
        at_slot = [slot == k for k in range(slots)]
        for c in range(3):
            out = jnp.zeros((8, LANES), F32)
            for k in range(slots):
                row = base + c * slots + k
                out = jnp.where(at_slot[k], row_gather(rows_ref[row:row + 1, :], peer, (8, LANES)), out)
            yield c, out

    for m in range(MB // 8):
        for c, out in collect(SB + 8 * m, 3 * SK, MK):
            own_ref[c, 8 * m:8 * m + 8] = out

    sub = iota((32, LANES), 0)
    comp = sub % 3
    node = sub // 3
    zero = jnp.zeros((64, LANES), BF16)
    both = jnp.zeros((8 * 64, 2 * LANES), F32)
    left, right = [], []
    for r in range(MB):
        f = jnp.where(comp == 0, own_ref[0, r:r + 1, :], own_ref[1, r:r + 1, :])
        f = jnp.where(comp == 2, own_ref[2, r:r + 1, :], f)
        f = jnp.where(node == mnode_ref[r:r + 1, :], f, 0.0)
        f = jnp.concatenate(split(f), 0)
        face = mface_ref[r:r + 1, :]
        high = wide16(face >> 8, 64)
        left.append(jnp.concatenate(
            [jnp.where(high == jnp.full((64, LANES), h, I16), f, zero) for h in range(8)], 0
        ))
        right.append(one_hot(2 * LANES, face & 255))
        if r % 2 == 1:
            both = both + dot_nt(jnp.concatenate(left, 1), jnp.concatenate(right, 1))
            left, right = [], []
    for h in range(8):
        at = slice(h * 256, (h + 1) * 256)
        share = both[64 * h:64 * h + 32] + both[64 * h + 32:64 * h + 64]
        face_ref[:, at] = (part_ref[:, at] + share)[0:27]

    for m in range(SB // 8):
        for c, out in collect(8 * m, 0, SK):
            for r in range(8):
                at = (8 * m + r) * LANES
                slave_ref[c:c + 1, at:at + LANES] = out[r:r + 1, :]


def finish(back, keys, mface, mnode, part):
    return call(
        finish_body,
        (
            jax.ShapeDtypeStruct((3, SB * LANES), F32),
            jax.ShapeDtypeStruct((27, FT * LANES), F32),
        ),
        [
            pltpu.VMEM((3 * LANES, LANES), F32),
            pltpu.VMEM((3, MB, LANES), F32),
        ],
        cost=10**9,
    )(back, keys, mface, mnode, part)


def exchange(x):
    x = x.reshape(DEV, 1, 3 * LANES)
    x = lax.all_to_all(x, ("mech", "bin"), split_axis=0, concat_axis=0, tiled=True)
    return x.reshape(3 * DEV, LANES)


def shards(
    face_coords, face_stiff, bin_order, slave_pos, slave_dest, face_slot, block_count,
    mirror_face, mirror_node, mirror_dest, mirror_slot,
):
    mface = mirror_face.reshape(MB, LANES)
    mnode = mirror_node.reshape(MB, LANES)
    send, keys = pack(
        block_count,
        slave_dest.reshape(SB, LANES),
        face_slot.reshape(SB, LANES),
        slave_pos,
        mirror_dest.reshape(MB, LANES),
        mirror_slot.reshape(MB, LANES),
        mface,
        mnode,
        face_coords,
    )
    recv = exchange(send)
    table, inv = order_faces(
        face_coords, face_stiff.reshape(1, FT * LANES), bin_order.reshape(FT, LANES)
    )
    back, uv, force, index = forces(recv, table)
    returned = exchange(back)
    part = react(uv, force, index, inv)
    return finish(returned, keys, mface, mnode, part)


def solution(mesh):
    axes = ("mech", "bin")
    return jax.shard_map(
        shards,
        mesh=mesh,
        in_specs=(
            P(None, axes), P(axes), P(axes, None), P(None, axes), P(axes, None), P(axes),
            P(axes, None), P(axes), P(axes), P(axes, None), P(axes),
        ),
        out_specs=(P(None, axes), P(None, axes)),
        check_vma=False,
    )
```

```python
import functools

import jax
import jax.numpy as jnp
from jax import lax
from jax.experimental import pallas as pl
from jax.experimental.pallas import tpu as pltpu
from jax.sharding import PartitionSpec as P

NEWTON = 5
CLIP_EDGE = 1.1
VMEM_BYTES = 16 * 2**20
F32 = jnp.float32
BF16 = jnp.bfloat16
I32 = jnp.int32
I16 = jnp.int16
LANES = 128
SB = 32
MB = 16
FT = 16
DEV = 128
NBIN = 8
SK = 64
MK = 32


def iota(shape, dim):
    return lax.broadcasted_iota(I32, shape, dim)


def dot_nt(a, b):
    return lax.dot_general(a, b, (((1,), (1,)), ((), ())), preferred_element_type=F32)


def wide16(row, rows):
    narrow = jnp.broadcast_to(row, (16, LANES)).astype(I16)
    return jnp.concatenate([narrow] * (rows // 16), 0) if rows > 16 else narrow


def slot_rows(rows):
    return iota((rows, LANES), 0).astype(I16)


def pick_bf16(rows16, row):
    hit = rows16 == wide16(row, rows16.shape[0])
    return jnp.where(hit, jnp.ones(rows16.shape, BF16), jnp.zeros(rows16.shape, BF16))


def one_hot(rows, row):
    return pick_bf16(slot_rows(rows), row)


def row_gather(row, lane, shape):
    return jnp.take_along_axis(jnp.broadcast_to(row, shape), lane, axis=1)


def call(body, out_shape, scratch=(), in_specs=None, cost=0, vmem=VMEM_BYTES):
    kwargs = {} if in_specs is None else {"in_specs": in_specs}
    return pl.pallas_call(
        body,
        out_shape=out_shape,
        scratch_shapes=list(scratch),
        compiler_params=pltpu.CompilerParams(vmem_limit_bytes=vmem),
        cost_estimate=pl.CostEstimate(flops=cost, bytes_accessed=cost // 100, transcendentals=0),
        **kwargs,
    )


VM = pl.BlockSpec(memory_space=pltpu.VMEM)
HB = pl.BlockSpec(memory_space=pltpu.HBM)


def pack_body(*refs):
    sources, send_ref, keys_ref, buffers, refs = refs[:9], refs[9], refs[10], refs[11:20], refs[20:]
    coords_ref, spos_ref, sdest_ref, sslot_ref, mdest_ref, mslot_ref, mface_ref, mnode_ref, count_ref = buffers
    e_ref, b_ref, val_ref, parts_ref, turn_ref, cols_ref, cnt_ref, rows_ref, sems = refs
    copies = [
        pltpu.make_async_copy(sources[i], buffers[i], sems.at[i]) for i in range(9)
    ]
    for copy in copies:
        copy.start()
    for copy in copies:
        copy.wait()

    def keys(dest, slot):
        owner = (dest & ~(NBIN - 1)) | (slot >> 8)
        return owner, dest & (NBIN - 1), (slot & 255) + 1

    half = LANES // 2
    for first, rows, dest_ref, slot_ref in ((0, SB, sdest_ref, sslot_ref), (SB, MB, mdest_ref, mslot_ref)):
        owner, col, code = keys(dest_ref[...], slot_ref[...])
        e_ref[first:first + rows] = owner
        b_ref[first:first + rows] = col
        val_ref[6, first:first + rows] = code.astype(F32)
        keys_ref[first:first + rows] = owner
        cell = (owner * NBIN + col).astype(F32)
        turn_ref[first:first + rows] = cell
        turn_ref[half + first:half + first + rows] = pltpu.roll(cell, half, axis=1)
    for first in (SB + MB, half + SB + MB):
        turn_ref[first:first + half - SB - MB] = jnp.zeros((half - SB - MB, LANES), F32)
    cols_ref[...] = turn_ref[...].T

    lane_row = iota((1, LANES), 1)
    lane8 = iota((NBIN, LANES), 1)
    earlier = iota((half, LANES), 0) < (iota((half, LANES), 1) & (half - 1))
    sub8 = iota((NBIN, LANES), 0)
    upper = lane8 >= half
    row16 = iota((16, LANES), 0)
    bin_rows = jnp.where((row16 < 8) | (iota((16, LANES), 1) < half), row16 & 7, -1).astype(I16)

    for r in range(SB + MB):
        bins = pick_bf16(bin_rows, b_ref[r:r + 1, :])
        cnt_ref[r] = dot_nt(bins, one_hot(LANES, e_ref[r:r + 1, :]))

    for m in range(MB // 8):
        face = mface_ref[8 * m:8 * m + 8]
        tile = face >> 7
        lane = face & 127
        node = mnode_ref[8 * m:8 * m + 8]
        at_tile = [tile == t for t in range(FT)]
        for c in range(3):
            point = jnp.zeros((8, LANES), F32)
            for n in range(9):
                part = jnp.zeros((8, LANES), F32)
                for t in range(FT):
                    got = row_gather(
                        coords_ref[3 * n + c:3 * n + c + 1, t * LANES:(t + 1) * LANES], lane, (8, LANES)
                    )
                    part = jnp.where(at_tile[t], got, part)
                point = jnp.where(node == n, part, point)
            high = point.astype(BF16).astype(F32)
            val_ref[c, SB + 8 * m:SB + 8 * m + 8] = high
            val_ref[3 + c, SB + 8 * m:SB + 8 * m + 8] = point - high

    x = spos_ref[...]
    high = x.astype(BF16).astype(F32)
    parts_ref[0] = high
    parts_ref[1] = x - high

    def value(i, r):
        if r >= SB or i == 6:
            return val_ref[i, r:r + 1, :]
        return parts_ref[i // 3, i % 3:i % 3 + 1, r * LANES:(r + 1) * LANES]

    def slots(first, last, cap, rows, base):
        seen = jnp.zeros((NBIN, LANES), F32)
        total = jnp.zeros((7 * rows, 2 * LANES), F32)
        zero = jnp.zeros((rows, LANES), BF16)
        for group in range(first, last, 4):
            left, right = [], []
            for r in range(group, group + 4):
                i = r - first
                peers = jnp.broadcast_to(e_ref[r:r + 1, :], (NBIN, LANES))
                column = jnp.where(upper, half + r, r)
                before = jnp.take_along_axis(seen, peers, axis=1) + jnp.where(
                    upper, jnp.take_along_axis(cnt_ref[r, 8:16], peers, axis=1), 0.0
                )
                before = jnp.where(sub8 == b_ref[r:r + 1, :], before, 0.0)
                for m in range(half // 8):
                    col = jnp.take_along_axis(cols_ref[8 * m:8 * m + 8], column, axis=1)
                    same = (turn_ref[r:r + 1, :] == col) & earlier[8 * m:8 * m + 8]
                    before = before + jnp.where(same, 1.0, 0.0)
                rank = jnp.sum(before, 0, keepdims=True)
                k = b_ref[r:r + 1, :] * cap + rank.astype(I32)
                place = k & (rows - 1)
                if first == 0:
                    live = lane_row < count_ref[0, i]
                    k = jnp.where(live, k, -1)
                    place = jnp.where(live, place, -1)
                keys_ref[SB + MB + r:SB + MB + r + 1, :] = k
                mine = slot_rows(rows) == wide16(place, rows)
                parts = []
                for j in (0, 1, 2, 6, 3, 4, 5):
                    x = jnp.broadcast_to(value(j, r), (16, LANES)).astype(BF16)
                    x = jnp.concatenate([x] * (rows // 16), 0) if rows > 16 else x
                    parts.append(jnp.where(mine, x, zero))
                left.append(jnp.concatenate(parts, 0))
                right.append(one_hot(2 * LANES, e_ref[r:r + 1, :] + jnp.where(k >= rows, LANES, 0)))
                seen = seen + cnt_ref[r, 0:8]
            total = total + dot_nt(jnp.concatenate(left, 1), jnp.concatenate(right, 1))
        for c in range(4):
            for h in range(2):
                lanes = slice(h * LANES, (h + 1) * LANES)
                out = total[c * rows:(c + 1) * rows, lanes]
                if c < 3:
                    out = out + total[(4 + c) * rows:(5 + c) * rows, lanes]
                at = base + (2 * c + h) * rows
                rows_ref[at:at + rows] = out

    slots(0, SB, 8, SK // 2, 0)
    slots(SB, SB + MB, 4, MK // 2, 4 * SK)
    for i in range(3):
        send_ref[pl.ds(i, DEV, stride=3), :] = rows_ref[i * LANES:(i + 1) * LANES].T


def pack(count, sdest, sslot, spos, mdest, mslot, mface, mnode, coords):
    blocks = SB + MB
    arrays = (coords, spos, sdest, sslot, mdest, mslot, mface, mnode)
    return call(
        pack_body,
        (
            jax.ShapeDtypeStruct((3 * DEV, LANES), F32),
            jax.ShapeDtypeStruct((2 * blocks, LANES), I32),
        ),
        [pltpu.VMEM(x.shape, x.dtype) for x in arrays] + [
            pltpu.SMEM(count.shape, I32),
            pltpu.VMEM((blocks, LANES), I32),
            pltpu.VMEM((blocks, LANES), I32),
            pltpu.VMEM((7, blocks, LANES), F32),
            pltpu.VMEM((2,) + spos.shape, F32),
            pltpu.VMEM((LANES, LANES), F32),
            pltpu.VMEM((LANES, LANES), F32),
            pltpu.VMEM((blocks, 16, LANES), F32),
            pltpu.VMEM((3 * LANES, LANES), F32),
            pltpu.SemaphoreType.DMA((9,)),
        ],
        in_specs=[HB] * 9,
        cost=10**9,
        vmem=60 * 1024 * 1024,
    )(*arrays, count)


def quadratic(low, mid, high):
    return mid, 0.5 * (high - low), 0.5 * (high + low) - mid


def order_body(coords_ref, stiff_ref, order_ref, table_ref, inv_ref, src_ref):
    for c in range(3):
        node = [coords_ref[3 * a + c:3 * a + c + 1, :] for a in range(9)]
        by_j = [quadratic(*node[3 * j:3 * j + 3]) for j in range(3)]
        for p in range(3):
            for q, value in enumerate(quadratic(by_j[0][p], by_j[1][p], by_j[2][p])):
                row = 9 * c + 3 * p + q
                src_ref[row:row + 1] = value
    src_ref[27:28] = stiff_ref[...]
    src_ref[28:32] = jnp.zeros((4, FT * LANES), F32)
    lanes_bf = iota((FT, LANES), 1).astype(F32).astype(BF16)
    zero = jnp.zeros((FT, LANES), BF16)
    inverse = jnp.zeros((2 * FT, LANES), F32)
    left, right = [], []
    for m in range(FT):
        order = order_ref[m:m + 1, :]
        hi = order >> 7
        lo = order & 127
        lane = jnp.broadcast_to(lo, (8, LANES))
        tile = jnp.broadcast_to(hi, (8, LANES))
        at_tile = [tile == t for t in range(FT)]
        for g in range(4):
            out = jnp.zeros((8, LANES), F32)
            for t in range(FT):
                got = jnp.take_along_axis(
                    src_ref[8 * g:8 * g + 8, t * LANES:(t + 1) * LANES], lane, axis=1
                )
                out = jnp.where(at_tile[t], got, out)
            table_ref[8 * g:8 * g + 8, m * LANES:(m + 1) * LANES] = out
        mine = slot_rows(FT) == wide16(hi, FT)
        left.append(jnp.concatenate([
            jnp.where(mine, jnp.full((FT, LANES), m, BF16), zero), jnp.where(mine, lanes_bf, zero)
        ], 0))
        right.append(one_hot(LANES, lo))
        if m % 4 == 3:
            inverse = inverse + dot_nt(jnp.concatenate(left, 1), jnp.concatenate(right, 1))
            left, right = [], []
    inv_ref[...] = inverse.astype(I32)


def order_faces(coords, stiff, order):
    faces = FT * LANES
    return call(
        order_body,
        (
            jax.ShapeDtypeStruct((32, faces), F32),
            jax.ShapeDtypeStruct((2 * FT, LANES), I32),
        ),
        [pltpu.VMEM((32, faces), F32)],
        cost=10**9,
    )(coords, stiff, order)


def project(point, coef, stiff):
    def with_slope(t, low, mid, high):
        top = high * t
        both = mid + top
        return low + t * both, both + top

    def surface(u, v):
        x, tu, tv = [], [], []
        for c in range(3):
            k = coef[c]
            along = [with_slope(u, k[0][q], k[1][q], k[2][q]) for q in range(3)]
            value, slope = with_slope(v, *[h for h, _ in along])
            d = [slope_u for _, slope_u in along]
            x.append(value)
            tu.append(d[0] + v * (d[1] + v * d[2]))
            tv.append(slope)
        return x, tu, tv

    def inner(a, b):
        return a[0] * b[0] + a[1] * b[1] + a[2] * b[2]

    u = v = jnp.zeros_like(point[0])
    for step in range(NEWTON):
        if step == 0:
            x = [coef[c][0][0] for c in range(3)]
            tu = [coef[c][1][0] for c in range(3)]
            tv = [coef[c][0][1] for c in range(3)]
        else:
            x, tu, tv = surface(u, v)
        o = [point[c] - x[c] for c in range(3)]
        a_uu, a_uv, a_vv = inner(tu, tu), inner(tu, tv), inner(tv, tv)
        b_u, b_v = inner(tu, o), inner(tv, o)
        scale = 1.0 / (a_uu * a_vv - a_uv * a_uv)
        du = (a_vv * b_u - a_uv * b_v) * scale
        dv = (a_uu * b_v - a_uv * b_u) * scale
        u = jnp.clip(u + du, -CLIP_EDGE, CLIP_EDGE)
        v = jnp.clip(v + dv, -CLIP_EDGE, CLIP_EDGE)
    x, tu, tv = surface(u, v)
    n = [
        tu[1] * tv[2] - tu[2] * tv[1],
        tu[2] * tv[0] - tu[0] * tv[2],
        tu[0] * tv[1] - tu[1] * tv[0],
    ]
    unit = 1.0 / jnp.sqrt(inner(n, n))
    gap = inner([point[c] - x[c] for c in range(3)], n) * unit
    size = 0.5 * stiff * jnp.maximum(-gap, 0.0) * unit
    return u, v, [size * n[c] for c in range(3)]


def force_body(recv_ref, table_ref, back_ref, uv_ref, force_ref, index_ref, rows_ref):
    for i in range(3):
        rows_ref[i * LANES:(i + 1) * LANES] = recv_ref[pl.ds(i, DEV, stride=3), :].T
    shape = (8, LANES)
    upper = iota(shape, 0) < 4
    force_ref[3 * SK + 3 * MK:] = jnp.zeros((LANES - 32, LANES), F32)
    for g in range(12):
        if g < 8:
            at = [c * SK + g * 8 for c in range(4)]
            out = [c * SK + g * 8 for c in range(3)]
        else:
            at = [4 * SK + c * MK + (g - 8) * 8 for c in range(4)]
            out = [3 * SK + c * MK + (g - 8) * 8 for c in range(3)]
        point = [rows_ref[at[c]:at[c] + 8, :] for c in range(3)]
        code = rows_ref[at[3]:at[3] + 8, :].astype(I32)
        index = jnp.maximum(code - 1, 0)
        lane = index & 127
        high = index >= LANES

        def entry(row, half):
            def tile(t):
                return jnp.broadcast_to(table_ref[row:row + 1, t * LANES:(t + 1) * LANES], shape)

            if g < 8:
                return tile(2 * g + half)
            first = 4 * (g - 8)
            return jnp.where(upper, tile(first + half), tile(first + 2 + half))

        def pick(row):
            got = [jnp.take_along_axis(entry(row, half), lane, axis=1) for half in range(2)]
            return jnp.where(high, got[1], got[0])

        coef = [[[pick(9 * c + 3 * p + q) for q in range(3)] for p in range(3)] for c in range(3)]
        stiff = jnp.where(code > 0, pick(27), 0.0)
        u, v, force = project(point, coef, stiff)
        uv_ref[g * 8:g * 8 + 8] = u
        uv_ref[96 + g * 8:96 + g * 8 + 8] = v
        index_ref[g * 8:g * 8 + 8] = index
        for c in range(3):
            force_ref[out[c]:out[c] + 8] = force[c]
    for i in range(3):
        back_ref[pl.ds(i, DEV, stride=3), :] = force_ref[i * LANES:(i + 1) * LANES].T


def forces(recv, table):
    return call(
        force_body,
        (
            jax.ShapeDtypeStruct((3 * DEV, LANES), F32),
            jax.ShapeDtypeStruct((192, LANES), F32),
            jax.ShapeDtypeStruct((3 * LANES, LANES), F32),
            jax.ShapeDtypeStruct((96, LANES), I32),
        ),
        [pltpu.VMEM((3 * LANES, LANES), F32)],
        cost=10**9,
    )(recv, table)


def split(x):
    high = x.astype(BF16)
    return high, (x - high.astype(F32)).astype(BF16)


def react_body(uv_ref, force_ref, index_ref, inv_ref, out_ref, part_ref, sum_ref):
    part_ref[27 * 8:] = jnp.zeros((40, LANES), F32)

    def pieces(g, first, count):
        left, right = [], []
        for k in range(first, first + count):
            left.append(jnp.concatenate(split(part_ref[pl.ds(k, 32, stride=8), :]), 0))
            right.append(one_hot(2 * LANES, index_ref[g * 8 + k:g * 8 + k + 1, :]))
        return dot_nt(jnp.concatenate(left, 1), jnp.concatenate(right, 1))

    def reactions(g):
        u = uv_ref[g * 8:g * 8 + 8]
        v = uv_ref[96 + g * 8:96 + g * 8 + 8]
        lu = (u * (u - 1.0) * 0.5, 1.0 - u * u, u * (u + 1.0) * 0.5)
        lv = (v * (v - 1.0) * 0.5, 1.0 - v * v, v * (v + 1.0) * 0.5)
        for c in range(3):
            row = c * SK + g * 8 if g < 8 else 3 * SK + c * MK + (g - 8) * 8
            f = -force_ref[row:row + 8]
            for j in range(3):
                fj = f * lv[j]
                for i in range(3):
                    a = 3 * (i + 3 * j) + c
                    part_ref[a * 8:a * 8 + 8] = lu[i] * fj

    mirrored = []
    for m in range(4):
        reactions(8 + m)
        mirrored += [pieces(8 + m, 0, 4), pieces(8 + m, 4, 4)]
        for b in (2 * m, 2 * m + 1):
            reactions(b)
            both = mirrored[b] + pieces(b, 0, 8)
            sum_ref[:, b * 256:(b + 1) * 256] = both[0:32] + both[32:64]

    for m in range(FT):
        hi = inv_ref[m:m + 1, :]
        lane = jnp.broadcast_to(inv_ref[FT + m:FT + m + 1, :], (8, LANES))
        tile = jnp.broadcast_to(hi, (8, LANES))
        at_tile = [tile == t for t in range(FT)]
        for g in range(4):
            out = jnp.zeros((8, LANES), F32)
            for t in range(FT):
                got = jnp.take_along_axis(
                    sum_ref[8 * g:8 * g + 8, t * LANES:(t + 1) * LANES], lane, axis=1
                )
                out = jnp.where(at_tile[t], got, out)
            out_ref[8 * g:8 * g + 8, m * LANES:(m + 1) * LANES] = out


def react(uv, force, index, inv):
    return call(
        react_body,
        jax.ShapeDtypeStruct((32, FT * LANES), F32),
        [
            pltpu.VMEM((256, LANES), F32),
            pltpu.VMEM((32, FT * LANES), F32),
        ],
        cost=10**9,
    )(uv, force, index, inv)


def finish_body(
    back_ref, keys_ref, mface_ref, mnode_ref, part_ref,
    slave_ref, face_ref, rows_ref, own_ref,
):
    for i in range(3):
        rows_ref[i * LANES:(i + 1) * LANES] = back_ref[pl.ds(i, DEV, stride=3), :].T

    def collect(block, base, slots):
        peer = keys_ref[block:block + 8]
        slot = keys_ref[SB + MB + block:SB + MB + block + 8]
        at_slot = [slot == k for k in range(slots)]
        for c in range(3):
            out = jnp.zeros((8, LANES), F32)
            for k in range(slots):
                row = base + c * slots + k
                out = jnp.where(at_slot[k], row_gather(rows_ref[row:row + 1, :], peer, (8, LANES)), out)
            yield c, out

    for m in range(MB // 8):
        for c, out in collect(SB + 8 * m, 3 * SK, MK):
            own_ref[c, 8 * m:8 * m + 8] = out

    sub = iota((32, LANES), 0)
    comp = sub % 3
    node = sub // 3
    zero = jnp.zeros((64, LANES), BF16)
    both = jnp.zeros((8 * 64, 2 * LANES), F32)
    left, right = [], []
    for r in range(MB):
        f = jnp.where(comp == 0, own_ref[0, r:r + 1, :], own_ref[1, r:r + 1, :])
        f = jnp.where(comp == 2, own_ref[2, r:r + 1, :], f)
        f = jnp.where(node == mnode_ref[r:r + 1, :], f, 0.0)
        f = jnp.concatenate(split(f), 0)
        face = mface_ref[r:r + 1, :]
        high = wide16(face >> 8, 64)
        left.append(jnp.concatenate(
            [jnp.where(high == jnp.full((64, LANES), h, I16), f, zero) for h in range(8)], 0
        ))
        right.append(one_hot(2 * LANES, face & 255))
        if r % 2 == 1:
            both = both + dot_nt(jnp.concatenate(left, 1), jnp.concatenate(right, 1))
            left, right = [], []
    for h in range(8):
        at = slice(h * 256, (h + 1) * 256)
        share = both[64 * h:64 * h + 32] + both[64 * h + 32:64 * h + 64]
        face_ref[:, at] = (part_ref[:, at] + share)[0:27]

    for m in range(SB // 8):
        for c, out in collect(8 * m, 0, SK):
            for r in range(8):
                at = (8 * m + r) * LANES
                slave_ref[c:c + 1, at:at + LANES] = out[r:r + 1, :]


def finish(back, keys, mface, mnode, part):
    return call(
        finish_body,
        (
            jax.ShapeDtypeStruct((3, SB * LANES), F32),
            jax.ShapeDtypeStruct((27, FT * LANES), F32),
        ),
        [
            pltpu.VMEM((3 * LANES, LANES), F32),
            pltpu.VMEM((3, MB, LANES), F32),
        ],
        cost=10**9,
    )(back, keys, mface, mnode, part)


def exchange(x):
    x = x.reshape(DEV, 1, 3 * LANES)
    x = lax.all_to_all(x, ("mech", "bin"), split_axis=0, concat_axis=0, tiled=True)
    return x.reshape(3 * DEV, LANES)


def shards(
    face_coords, face_stiff, bin_order, slave_pos, slave_dest, face_slot, block_count,
    mirror_face, mirror_node, mirror_dest, mirror_slot,
):
    mface = mirror_face.reshape(MB, LANES)
    mnode = mirror_node.reshape(MB, LANES)
    send, keys = pack(
        block_count,
        slave_dest.reshape(SB, LANES),
        face_slot.reshape(SB, LANES),
        slave_pos,
        mirror_dest.reshape(MB, LANES),
        mirror_slot.reshape(MB, LANES),
        mface,
        mnode,
        face_coords,
    )
    recv = exchange(send)
    table, inv = order_faces(
        face_coords, face_stiff.reshape(1, FT * LANES), bin_order.reshape(FT, LANES)
    )
    back, uv, force, index = forces(recv, table)
    returned = exchange(back)
    part = react(uv, force, index, inv)
    return finish(returned, keys, mface, mnode, part)


def solution(mesh):
    axes = ("mech", "bin")
    return jax.shard_map(
        shards,
        mesh=mesh,
        in_specs=(
            P(None, axes), P(axes), P(axes, None), P(None, axes), P(axes, None), P(axes),
            P(axes, None), P(axes), P(axes), P(axes, None), P(axes),
        ),
        out_specs=(P(None, axes), P(None, axes)),
        check_vma=False,
    )
```
